32 devices in a mesh: lat: 8 (over z, core), lon: 4 (over y, x).
Axes of the slice: x: 2, y: 2, z: 4, core: 2. Of those that a mesh axis runs over, the one named last changes fastest.
Arguments:
- misfit: float32 [8, 256, 512], P(None, 'lat', 'lon'), may hold values from -6 to 6
- flow_east: float32 [8, 256, 512], P(None, 'lat', 'lon'), may hold values from -6 to 6
- flow_north: float32 [8, 256, 512], P(None, 'lat', 'lon'), may hold values from -6 to 6
- ocean_depth: float32 [256, 512], P('lat', 'lon'), may hold values from 0.4 to 1.6
- drag_rate: float32 [256, 512], P('lat', 'lon'), may hold values from 0.02 to 0.3
- wet_mask: int32 [256, 512], P('lat', 'lon'), may hold values from 0 to 1, as said below
- legendre: bfloat16 [256, 256, 1024], P(('lon', 'lat')), as said below
- love_factor: float32 [256], replicated, may hold values from 0.2 to 2
- assignment: int32 [256], replicated, may hold values from 0 to 255, as said below
Outputs:
- adjoint_height: float32 [8, 256, 512], P(None, 'lat', 'lon')
- adjoint_east: float32 [8, 256, 512], P(None, 'lat', 'lon')
- adjoint_north: float32 [8, 256, 512], P(None, 'lat', 'lon')
The draws below stay inside these ranges and needn't reach their ends.
Inputs may be any that keep to these rules, and one draw needn't show every extreme that they name: `wet_mask`: 1 marks a wet cell and 0 land; the first and the last latitude rows are land. `assignment`: A permutation: each of the 256 orders appears once. `legendre`: entry [p, a, n] belongs to degree assignment[p] + n and is zero where assignment[p] + n >= 256.
All inputs are finite; a program needn't handle non-finite values.
Results may differ from the reference program's by a relative error of at most 0.0028.
Values may be sent and summed in bfloat16 or wider, within the bound.
A program may use at most 64 MiB of HBM per device.

```python
import math
import jax
import jax.numpy as jnp
from jax import lax

FIELDS = 8
DEGREES = 1024
TIME_STEPS = 4
LATITUDES = 256
LONGITUDES = 512
ORDERS = 256


def shared_order(key):
    return jax.random.permutation(jax.random.fold_in(key, 11), ORDERS).astype(jnp.int32)


def draw_assignment(key, part):
    return shared_order(key)


def draw_legendre(key, part):
    order_table = shared_order(key)
    table_key = jax.random.fold_in(key, 23)
    spread = float(LONGITUDES * LONGITUDES * LATITUDES * DEGREES) ** (-0.25)
    shape_full = (ORDERS, LATITUDES, DEGREES)
    values = jax.random.normal(table_key, shape_full, jnp.float32)
    degree_index = jnp.arange(DEGREES, dtype=jnp.int32)
    inside = order_table[:, None, None] + degree_index[None, None, :] < ORDERS
    return jnp.where(inside, values * spread, 0.0).astype(jnp.bfloat16)


def draw_wet_mask(key, part):
    cells = jax.random.randint(jax.random.fold_in(key, 3), (LATITUDES, LONGITUDES), 0, 4)
    row_index = jnp.arange(LATITUDES, dtype=jnp.int32)[:, None]
    wet_cells = (cells > 0) & (row_index > 0) & (row_index < LATITUDES - 1)
    return wet_cells.astype(jnp.int32)


def levels(key, shape, split, smallest, largest):
    def one(axis_at, shards_of):
        draws = jax.random.uniform(jax.random.fold_in(jax.random.fold_in(key, 6), axis_at), (shards_of,), jnp.float32, smallest / len(split), largest / len(split))
        return jnp.repeat(jnp.exp(draws), shape[axis_at] // shards_of).reshape((-1,) + (1,) * (len(shape) - axis_at - 1))

    loudness = one(*split[0])
    for cut in split[1:]:
        loudness = loudness * one(*cut)
    return loudness


def centred(rng, extent, scale, reach, cuts=(), kind=jnp.bfloat16):
    drawn = scale * jax.random.normal(rng, extent, jnp.float32)
    if cuts:
        drawn = drawn * levels(rng, extent, cuts, -0.22, 0.18)
    return jnp.clip(drawn, -reach, reach).astype(kind)


def setup_inputs(seed: int = 0) -> dict:
    keys = jax.random.split(jax.random.key(seed), 10)
    return {
        "misfit": centred(keys[0], (FIELDS, LATITUDES, LONGITUDES), 1.0, 6.0, ((1, 8), (2, 4)), jnp.float32),
        "flow_east": centred(keys[1], (FIELDS, LATITUDES, LONGITUDES), 1.0, 6.0, ((1, 8), (2, 4)), jnp.float32),
        "flow_north": centred(keys[2], (FIELDS, LATITUDES, LONGITUDES), 1.0, 6.0, ((1, 8), (2, 4)), jnp.float32),
        "ocean_depth": jnp.clip(jnp.exp(math.log(1.6) - 1.3862944 * jax.random.uniform(keys[3], (LATITUDES, LONGITUDES), jnp.float32) ** levels(keys[3], (LATITUDES, LONGITUDES), ((0, 8), (1, 4)), -0.2, 0.2)), 0.4, 1.6),
        "drag_rate": jnp.clip(jnp.exp(math.log(0.3) - 2.7080503 * jax.random.uniform(keys[4], (LATITUDES, LONGITUDES), jnp.float32) ** levels(keys[4], (LATITUDES, LONGITUDES), ((0, 8), (1, 4)), -0.2, 0.2)), 0.02, 0.3),
        "wet_mask": draw_wet_mask(jax.random.fold_in(keys[9], 71), 0),
        "legendre": draw_legendre(jax.random.fold_in(keys[9], 71), 0),
        "love_factor": jnp.clip(jnp.exp(jax.random.uniform(keys[7], (ORDERS,), jnp.float32, math.log(0.2), math.log(2.0))), 0.2, 2.0),
        "assignment": draw_assignment(jax.random.fold_in(keys[9], 71), 0),
    }


def shifted_diffs(field):
    east_diff = jnp.roll(field, -1, axis=2) - jnp.roll(field, 1, axis=2)
    padded = jnp.pad(field, ((0, 0), (1, 1), (0, 0)))
    north_diff = padded[:, 2:, :] - padded[:, :-2, :]
    return east_diff, north_diff


def adjoint_step(height, east_flow, north_flow, wetness, ocean_depth, drag_rate):
    east_diff, north_diff = shifted_diffs(height)
    retained = 1.0 - drag_rate
    east_flow = wetness * (retained * east_flow - 0.5 * east_diff)
    north_flow = wetness * (retained * north_flow - 0.5 * north_diff)
    flow_east_diff, _ = shifted_diffs(east_flow)
    _, flow_north_diff = shifted_diffs(north_flow)
    height = wetness * (height - 0.5 * ocean_depth * (flow_east_diff + flow_north_diff))
    return height, east_flow, north_flow


def reference(misfit, flow_east, flow_north, ocean_depth, drag_rate, wet_mask, legendre, love_factor, assignment):
    wetness = wet_mask.astype(jnp.float32)
    height = wetness * misfit
    east_flow = wetness * flow_east
    north_flow = wetness * flow_north
    for _ in range(TIME_STEPS):
        height, east_flow, north_flow = adjoint_step(height, east_flow, north_flow, wetness, ocean_depth, drag_rate)
    spectrum = jnp.fft.rfft(height, axis=2)[:, :, :ORDERS]
    real_part = jnp.real(spectrum).astype(jnp.float32)
    imag_part = jnp.imag(spectrum).astype(jnp.float32)
    stacked = jnp.stack([real_part, imag_part], axis=0).astype(jnp.bfloat16)
    by_position = jnp.transpose(stacked, (3, 0, 1, 2))[assignment]
    love_pad = jnp.concatenate([love_factor, jnp.zeros((DEGREES,), love_factor.dtype)])

    def per_position(inputs):
        spectra_here, table_here, order_here = inputs
        factors = lax.dynamic_slice(love_pad, (order_here.astype(jnp.int32),), (DEGREES,))
        table_wide = table_here.astype(jnp.float32)
        coefficients = jnp.dot(spectra_here.reshape(2 * FIELDS, LATITUDES).astype(jnp.float32), table_wide)
        coefficients = (coefficients * factors[None, :]).astype(jnp.bfloat16)
        return jnp.dot(coefficients.astype(jnp.float32), table_wide.T).astype(jnp.bfloat16)

    synthesis = lax.map(per_position, (by_position, legendre, assignment))
    by_order = jnp.zeros_like(synthesis).at[assignment].set(synthesis)
    by_order = by_order.astype(jnp.float32).reshape(ORDERS, 2, FIELDS, LATITUDES)
    coeffs = lax.complex(by_order[:, 0], by_order[:, 1])
    coeffs = jnp.transpose(coeffs, (1, 2, 0))
    coeffs = jnp.pad(coeffs, ((0, 0), (0, 0), (0, 1)))
    loading = (jnp.fft.irfft(coeffs, n=LONGITUDES, axis=2) * LONGITUDES).astype(jnp.float32)
    height = height + wetness * loading
    return adjoint_step(height, east_flow, north_flow, wetness, ocean_depth, drag_rate)
```

```python
import math

import jax
import jax.numpy as jnp
from jax import lax
from jax.experimental import pallas as pl
from jax.experimental.pallas import tpu as pltpu
from jax.sharding import PartitionSpec as P

TIME_STEPS = 4


TWO_PI = 2.0 * math.pi
exact_mode = lax.Precision.HIGHEST


def with_halo(cells, sides, width):
    for axis, dim in sides:
        count = lax.axis_size(axis)
        head = lax.slice_in_dim(cells, 0, width, axis=dim)
        tail = lax.slice_in_dim(cells, cells.shape[dim] - width, cells.shape[dim], axis=dim)
        cells = jnp.concatenate(
            [
                lax.ppermute(tail, axis, [(i, (i + 1) % count) for i in range(count)]),
                cells,
                lax.ppermute(head, axis, [((i + 1) % count, i) for i in range(count)]),
            ],
            axis=dim,
        )
    return cells


def extend(stacked):
    return with_halo(stacked, (("lat", 2), ("lon", 3)), 1)


def differences(extended):
    east_diff = extended[:, :, 1:-1, 2:] - extended[:, :, 1:-1, :-2]
    north_diff = extended[:, :, 2:, 1:-1] - extended[:, :, :-2, 1:-1]
    return (east_diff, north_diff)


def adjoint_step(height, east_flow, north_flow, wetness, ocean_depth, drag_rate):
    east_diff, north_diff = differences(extend(height[None]))
    retained = 1.0 - drag_rate
    east_flow = wetness * (retained * east_flow - 0.5 * east_diff[0])
    north_flow = wetness * (retained * north_flow - 0.5 * north_diff[0])
    flow_east_diff, flow_north_diff = differences(extend(jnp.stack([east_flow, north_flow])))
    height = wetness * (height - 0.5 * ocean_depth * (flow_east_diff[0] + flow_north_diff[1]))
    return (height, east_flow, north_flow)


def phases(orders, positions, period):
    products = orders[:, None] * positions[None, :] % period
    radians = products.astype(jnp.float32) * (TWO_PI / period)
    return (jnp.cos(radians), jnp.sin(radians))


def spherical(spectra, legendre, weights, lat_count, row_count):
    slot_count = legendre.shape[0]
    degree_count = legendre.shape[2]
    legendre_blocks = legendre.reshape(slot_count, lat_count, row_count, degree_count)
    spectra_blocks = spectra.reshape(slot_count, lat_count, -1, row_count)
    coefficients = jnp.einsum(
        "kicr,kirn->kcn", spectra_blocks, legendre_blocks, preferred_element_type=jnp.float32
    )
    coefficients = (coefficients * weights[:, None, :]).astype(jnp.bfloat16)
    synthesis = jnp.einsum(
        "kcn,kirn->kicr", coefficients, legendre_blocks, preferred_element_type=jnp.float32
    )
    return synthesis.astype(jnp.bfloat16)


def local(
    misfit,
    flow_east,
    flow_north,
    ocean_depth,
    drag_rate,
    wet_mask,
    legendre,
    love_factor,
    assignment,
):
    field_count, row_count, col_count = misfit.shape
    lat_count = lax.axis_size("lat")
    lon_count = lax.axis_size("lon")
    period = col_count * lon_count
    order_count = period // 2
    slot_count = legendre.shape[0]
    degree_count = legendre.shape[2]
    row_pair = row_count // lon_count
    lat_index = lax.axis_index("lat")
    lon_index = lax.axis_index("lon")
    wetness = wet_mask.astype(jnp.float32)
    height = wetness * misfit
    east_flow = wetness * flow_east
    north_flow = wetness * flow_north

    def advance(height, east_flow, north_flow):
        return adjoint_step(height, east_flow, north_flow, wetness, ocean_depth, drag_rate)

    for _ in range(TIME_STEPS):
        height, east_flow, north_flow = advance(height, east_flow, north_flow)
    base = (lon_index * lat_count + lat_index) * slot_count
    my_orders = lax.dynamic_slice_in_dim(assignment, base, slot_count)
    love_pad = jnp.concatenate([love_factor, jnp.zeros((degree_count,), jnp.float32)])
    weights = jax.vmap(
        lambda first_order: lax.dynamic_slice_in_dim(love_pad, first_order, degree_count)
    )(my_orders)
    all_cells = jnp.arange(period, dtype=jnp.int32)
    cos_full, sin_full = phases(assignment, all_cells, period)
    row_block = lax.all_to_all(height, "lon", split_axis=1, concat_axis=2, tiled=True)
    real_part = jnp.einsum("nrx,mx->nrm", row_block, cos_full, precision=exact_mode)
    imag_part = -jnp.einsum("nrx,mx->nrm", row_block, sin_full, precision=exact_mode)
    rowwise = jnp.stack([real_part, imag_part], 2).astype(jnp.bfloat16)
    gathered = rowwise.transpose(3, 2, 0, 1).reshape(lon_count, lat_count, -1)
    received = lax.all_to_all(
        lax.all_to_all(gathered, "lat", split_axis=1, concat_axis=1, tiled=True),
        "lon",
        split_axis=0,
        concat_axis=0,
        tiled=True,
    )
    received = received.reshape(lon_count, lat_count, slot_count, 2, field_count, row_pair)
    spectra = received.transpose(2, 1, 3, 4, 0, 5).reshape(
        slot_count, lat_count, 2 * field_count * row_count
    )
    synthesis = spherical(spectra, legendre, weights, lat_count, row_count)
    arranged = synthesis.reshape(slot_count, lat_count, 2, field_count, lon_count, row_pair)
    arranged = arranged.transpose(4, 1, 0, 2, 3, 5).reshape(lon_count, lat_count, -1)
    returned = lax.all_to_all(
        lax.all_to_all(arranged, "lat", split_axis=1, concat_axis=1, tiled=True),
        "lon",
        split_axis=0,
        concat_axis=0,
        tiled=True,
    )
    returned = returned.reshape(order_count, 2, field_count, row_pair).astype(jnp.float32)
    doubling = jnp.where(assignment == 0, 1.0, 2.0).astype(jnp.float32)
    grid_rows = jnp.einsum(
        "mx,mfr->frx", cos_full * doubling[:, None], returned[:, 0], precision=exact_mode
    ) - jnp.einsum(
        "mx,mfr->frx", sin_full * doubling[:, None], returned[:, 1], precision=exact_mode
    )
    loading = lax.all_to_all(grid_rows, "lon", split_axis=2, concat_axis=1, tiled=True)
    height = height + wetness * loading
    return advance(height, east_flow, north_flow)


EDGE = 8
MESH = pl.DeviceIdType.MESH


def turn(value, shift, axis):
    size = value.shape[axis]
    return pltpu.roll(value, shift % size, axis)


def step_on_tile(height, east, north, keep, half, depth):
    east_diff = turn(height, -1, 1) - turn(height, 1, 1)
    north_diff = turn(height, -1, 0) - turn(height, 1, 0)
    east = keep * east - half * east_diff
    north = keep * north - half * north_diff
    spread = (turn(east, -1, 1) - turn(east, 1, 1)) + (turn(north, -1, 0) - turn(north, 1, 0))
    return height - depth * spread, east, north


def unit_cosine(counts, period):
    part = (counts & (period - 1)).astype(jnp.float32) * (1.0 / period)
    angle = (jnp.abs(part - 0.5) - 0.25) * TWO_PI
    square = angle * angle
    series = -1.0 / 39916800.0
    for denominator in (362880.0, -5040.0, 120.0, -6.0, 1.0):
        series = series * square + 1.0 / denominator
    return series * angle


def split_pair(value):
    high = value.astype(jnp.bfloat16)
    return high, (value - high.astype(jnp.float32)).astype(jnp.bfloat16)


def swap_chunks(parts, width):
    count = len(parts)
    lane = lax.broadcasted_iota(jnp.int32, parts[0].shape, 1) // width
    parts = list(parts)
    distance = 1
    while distance < count:
        upper = (lane // distance) % 2 == 1
        for low in range(count):
            if (low // distance) % 2 == 0:
                first, second = parts[low], parts[low + distance]
                parts[low] = jnp.where(upper, turn(second, width * distance, 1), first)
                parts[low + distance] = jnp.where(upper, second, turn(first, -width * distance, 1))
        distance *= 2
    return parts


def fused_kernel(
    lat_count, lon_count, misfit, flow_east, flow_north, depth_in, drag_in, wet_in, table_in, love_in,
    order_in, out_h, out_u, out_w, table, pack, rlon, rlat, rdepth, rdrag, rwet, coef, stepped, gath,
    forward_table, inverse_table, order_col, weights, spec_out, spec_in, syn_out, syn, pack2, rlon2,
    rw2, total, rh3, loading, table_sem, lat_send, lat_recv, lon_send, lon_recv, diag_send, diag_recv,
    g_send, g_recv, a_send, a_recv, b_send, b_recv, c_send, c_recv, w_send, w_recv, p_send, p_recv,
    h_send, h_recv,
):
    fields, rows, cols = misfit.shape
    slots = table.shape[0]
    used = table.shape[2]
    period = cols * lon_count
    ext_rows, ext_cols = rows + 2 * EDGE, 2 * cols
    pair = 2 * slots
    lat, lon = lax.axis_index("lat"), lax.axis_index("lon")
    last = lat_count - 1
    has_up, has_down = lat > 0, lat < last
    left, right = lax.rem(lon + lon_count - 1, lon_count), lax.rem(lon + 1, lon_count)
    table_copy = pltpu.make_async_copy(table_in.at[:, :, pl.ds(0, used)], table, table_sem)
    table_copy.start()
    barrier = pltpu.get_barrier_semaphore()

    def hello(at_lat, at_lon):
        pl.semaphore_signal(barrier, inc=1, device_id={"lat": at_lat, "lon": at_lon}, device_id_type=MESH)

    @pl.when(lat == 0)
    def _():
        rlat[:, :, EDGE:, :] = jnp.zeros((3, fields, EDGE, cols), jnp.float32)
        rdepth[EDGE:, :] = jnp.zeros((EDGE, cols), jnp.float32)
        rdrag[EDGE:, :] = jnp.zeros((EDGE, cols), jnp.float32)
        rwet[EDGE:, :] = jnp.zeros((EDGE, cols), jnp.int32)
        rlon[:, :, rows + EDGE:, :] = jnp.zeros((2, 2, EDGE, cols), jnp.float32)
        rw2[:, EDGE:, :] = jnp.zeros((fields, EDGE, cols), jnp.float32)
        rh3[:, EDGE:, :] = jnp.zeros((fields, EDGE, cols), jnp.float32)

    @pl.when(lat == last)
    def _():
        rlat[:, :, :EDGE, :] = jnp.zeros((3, fields, EDGE, cols), jnp.float32)
        rdepth[:EDGE, :] = jnp.zeros((EDGE, cols), jnp.float32)
        rdrag[:EDGE, :] = jnp.zeros((EDGE, cols), jnp.float32)
        rwet[:EDGE, :] = jnp.zeros((EDGE, cols), jnp.int32)
        rlon[:, :, rows:rows + EDGE, :] = jnp.zeros((2, 2, EDGE, cols), jnp.float32)
        rw2[:, :EDGE, :] = jnp.zeros((fields, EDGE, cols), jnp.float32)
        rh3[:, :EDGE, :] = jnp.zeros((fields, EDGE, cols), jnp.float32)

    for d in range(1, lat_count):
        hello(lax.rem(lat + d, lat_count), lon)
    for d in range(1, lon_count):
        hello(lat, lax.rem(lon + d, lon_count))

    @pl.when(has_up)
    def _():
        hello(lat - 1, left)
        hello(lat - 1, right)

    @pl.when(has_down)
    def _():
        hello(lat + 1, left)
        hello(lat + 1, right)

    lane_own = lax.broadcasted_iota(jnp.int32, (rows, cols), 1)

    def pack_edges(groups, target):
        for t, group in enumerate(groups):
            heads = jnp.zeros((rows, cols), jnp.float32)
            tails = jnp.zeros((rows, cols), jnp.float32)
            for s, value in enumerate(group):
                here = lane_own // EDGE == s
                heads = jnp.where(here, turn(value, EDGE * s, 1), heads)
                tails = jnp.where(here, turn(value, EDGE * s + EDGE, 1), tails)
            target[0, t] = heads
            target[1, t] = tails

    pack_edges(
        (
            [misfit[f] for f in range(fields)] + [flow_east[f] for f in range(fields)],
            [flow_north[f] for f in range(fields)]
            + [depth_in[...], drag_in[...], wet_in[...].astype(jnp.float32)],
        ),
        pack,
    )
    sides = has_up.astype(jnp.int32) + has_down.astype(jnp.int32)
    pl.semaphore_wait(barrier, lat_count + lon_count - 2 + 2 * sides)

    def remote(source, target, send, recv, at_lat, at_lon):
        return pltpu.make_async_remote_copy(
            src_ref=source, dst_ref=target, send_sem=send, recv_sem=recv,
            device_id={"lat": at_lat, "lon": at_lon}, device_id_type=MESH,
        )

    def lat_copies(up):
        here = pl.ds(0, EDGE) if up else pl.ds(rows - EDGE, EDGE)
        there = pl.ds(0, EDGE) if up else pl.ds(EDGE, EDGE)
        at = lat - 1 if up else lat + 1
        k = 0 if up else 1
        pairs = [
            (misfit.at[:, here], rlat.at[0, :, there]),
            (flow_east.at[:, here], rlat.at[1, :, there]),
            (flow_north.at[:, here], rlat.at[2, :, there]),
            (depth_in.at[here], rdepth.at[there]),
            (drag_in.at[here], rdrag.at[there]),
            (wet_in.at[here], rwet.at[there]),
        ]
        copies = [
            remote(s, t, lat_send.at[k, n], lat_recv.at[k, n], at, lon) for n, (s, t) in enumerate(pairs)
        ]
        corner = pl.ds(rows, EDGE) if up else pl.ds(rows + EDGE, EDGE)
        for side, at_lon in ((0, left), (1, right)):
            n = 2 * k + side
            copies.append(
                remote(
                    pack.at[side, :, here], rlon.at[side, :, corner], diag_send.at[n], diag_recv.at[n], at, at_lon
                )
            )
        return copies

    lon_copies = [
        remote(pack.at[s], rlon.at[s, :, pl.ds(0, rows)], lon_send.at[s], lon_recv.at[s], lat, at)
        for s, at in ((0, left), (1, right))
    ]

    def on_sides(make, act_up, act_down):
        @pl.when(has_up)
        def _():
            for copy in make(True):
                act_up(copy)

        @pl.when(has_down)
        def _():
            for copy in make(False):
                act_down(copy)

    def start(copy):
        copy.start()

    def wait_send(copy):
        copy.wait_send()

    def wait_recv_sides(make):
        @pl.when(has_down)
        def _():
            for copy in make(True):
                copy.wait_recv()

        @pl.when(has_up)
        def _():
            for copy in make(False):
                copy.wait_recv()

    on_sides(lat_copies, start, start)
    for copy in lon_copies:
        copy.start()

    orders = period // 2
    span = 2 * orders
    row_id = lax.broadcasted_iota(jnp.int32, (span, orders), 0) // 2
    position_id = lax.broadcasted_iota(jnp.int32, (span, orders), 1)
    chosen = jnp.where(row_id == position_id, order_in[...].astype(jnp.float32), 0.0)
    order_col[...] = jnp.sum(chosen, axis=1, keepdims=True).astype(jnp.int32)

    block = lat_count * pair
    parity = (lax.broadcasted_iota(jnp.int32, (block, ext_cols), 0) % 2) * (period // 4)
    lane_ext = lax.broadcasted_iota(jnp.int32, (block, ext_cols), 1)
    shifted = jnp.where(lane_ext < cols + cols // 2, lane_ext, lane_ext - ext_cols) + lon * cols
    for j in range(lon_count):
        order_here = order_col[pl.ds(j * block, block), :]
        value = unit_cosine(order_here * shifted + parity, period)
        value = value * jnp.where(order_here == 0, 1.0, 2.0)
        inverse_table[0, j], inverse_table[1, j] = split_pair(value)
    mine = order_col[pl.ds(pl.multiple_of(lon * block, block), block), :]
    lane_full = lax.broadcasted_iota(jnp.int32, (block, cols), 1)
    for j in range(lon_count):
        value = unit_cosine(mine * (lane_full + j * cols) + parity[:, :cols], period)
        forward_table[j, 0:block], forward_table[j, block:] = split_pair(value)

    degree_row = lax.broadcasted_iota(jnp.int32, (orders, used), 0)
    degree_lane = lax.broadcasted_iota(jnp.int32, (orders, used), 1)
    diagonal = lax.broadcasted_iota(jnp.int32, (orders, orders), 0) == lax.broadcasted_iota(
        jnp.int32, (orders, orders), 1
    )
    love_col = jnp.sum(jnp.where(diagonal, love_in[...], 0.0), axis=1, keepdims=True)
    offset = degree_row - degree_lane
    first = (lon * lat_count + lat) * slots
    for p in range(slots):
        order_here = order_col[pl.ds(2 * (first + p), 1), :]
        weights[p:p + 1, :] = jnp.sum(jnp.where(offset == order_here, love_col, 0.0), axis=0, keepdims=True)

    wait_recv_sides(lat_copies)
    for copy in lon_copies:
        copy.wait_recv()

    lane_tall = lax.broadcasted_iota(jnp.int32, (ext_rows, cols), 1)

    def assemble(own, beside, ahead, behind, slot):
        main = jnp.concatenate([own, beside], axis=0)
        ahead = turn_to(ahead, cols - EDGE * slot)
        behind = turn_to(behind, 2 * cols - EDGE - EDGE * slot)
        extra = jnp.where(lane_tall < EDGE, ahead, jnp.where(lane_tall >= cols - EDGE, behind, 0.0))
        return jnp.concatenate([main, extra], axis=1)

    def turn_to(value, shift):
        return pltpu.roll(value, shift % cols if isinstance(shift, int) else lax.rem(shift, cols), 1)

    depth_ext = assemble(depth_in[...], rdepth[...], rlon[0, 1], rlon[1, 1], fields)
    drag_ext = assemble(drag_in[...], rdrag[...], rlon[0, 1], rlon[1, 1], fields + 1)
    wet_ext = assemble(
        wet_in[...].astype(jnp.float32), rwet[...].astype(jnp.float32), rlon[0, 1], rlon[1, 1], fields + 2
    )
    coef[0] = wet_ext * (1.0 - drag_ext)
    coef[1] = 0.5 * wet_ext
    coef[2] = 0.5 * wet_ext * depth_ext
    coef[3] = wet_ext

    @pl.loop(0, fields)
    def _(f):
        keep, half, depth, wet = coef[0], coef[1], coef[2], coef[3]
        height = wet * assemble(misfit[f], rlat[0, f], rlon[0, 0], rlon[1, 0], f)
        east = wet * assemble(flow_east[f], rlat[1, f], rlon[0, 0], rlon[1, 0], f + fields)
        north = wet * assemble(flow_north[f], rlat[2, f], rlon[0, 1], rlon[1, 1], f)
        for _ in range(TIME_STEPS):
            height, east, north = step_on_tile(height, east, north, keep, half, depth)
        height = height[:rows, :cols]
        stepped[0, f] = height
        stepped[1, f] = east[:rows, :cols]
        stepped[2, f] = north[:rows, :cols]
        gath[lon, pl.ds(pl.multiple_of(f * rows, rows), rows), :] = height.astype(jnp.bfloat16)

    def lon_gather(ref, send, recv):
        return [
            remote(ref.at[lon], ref.at[lon], send.at[d - 1], recv.at[d - 1], lat, lax.rem(lon + d, lon_count))
            for d in range(1, lon_count)
        ]

    def source(d):
        return lax.rem(lon + lon_count - d, lon_count)

    g_copies = lon_gather(gath, g_send, g_recv)
    for copy in g_copies:
        copy.start()

    pack_edges(([stepped[k, f] for k in range(2) for f in range(fields)],), pack2)

    def w_copies(up):
        here = pl.ds(0, EDGE) if up else pl.ds(rows - EDGE, EDGE)
        there = pl.ds(0, EDGE) if up else pl.ds(EDGE, EDGE)
        k = 0 if up else 1
        at = lat - 1 if up else lat + 1
        return [remote(stepped.at[2, :, here], rw2.at[:, there], w_send.at[k], w_recv.at[k], at, lon)]

    p_copies = [
        remote(pack2.at[s, 0], rlon2.at[s, pl.ds(0, rows)], p_send.at[s], p_recv.at[s], lat, at)
        for s, at in ((0, left), (1, right))
    ]

    def transform(j):
        return lax.dot_general(
            forward_table[j], gath[j], (((1,), (1,)), ((), ())), preferred_element_type=jnp.float32
        )

    both = transform(lon)
    for d in range(1, lon_count):
        g_copies[d - 1].wait_recv()
        both = both + transform(source(d))
    spectra = (both[:block] + both[block:]).astype(jnp.bfloat16)
    for i in range(lat_count):
        spec_out[i] = spectra[i * pair:(i + 1) * pair]

    def lat_exchange(ref, target, slot, send, recv):
        copies = []
        for d in range(1, lat_count):
            peer = lax.rem(lat + d, lat_count)
            copies.append(remote(ref.at[peer], slot, send.at[d - 1], recv.at[d - 1], peer, lon))
        return copies

    a_copies = lat_exchange(spec_out, spec_in, spec_in.at[lat], a_send, a_recv)
    for copy in a_copies:
        copy.start()
    on_sides(w_copies, start, start)
    for copy in p_copies:
        copy.start()
    spec_in[lat] = spec_out[lat]
    table_copy.wait()
    for copy in a_copies:
        copy.wait_recv()
    by_field = swap_chunks([spec_in[i].astype(jnp.float32) for i in range(lat_count)], rows)
    arranged = jnp.concatenate(by_field, axis=0).astype(jnp.bfloat16)
    slot_of_row = (lax.broadcasted_iota(jnp.int32, (fields * pair, used), 0) // 2) % slots
    coefficients = jnp.zeros((fields * pair, used), jnp.float32)
    for p in range(slots):
        product = jnp.dot(arranged, table[p], preferred_element_type=jnp.float32)
        coefficients = jnp.where(slot_of_row == p, product * weights[p:p + 1, :], coefficients)
    synthesis = jnp.zeros((fields * pair, table.shape[1]), jnp.float32)
    for p in range(slots):
        synthesis = synthesis + lax.dot_general(
            jnp.where(slot_of_row == p, coefficients, 0.0).astype(jnp.bfloat16),
            table[p],
            (((1,), (1,)), ((), ())),
            preferred_element_type=jnp.float32,
        )
    by_lat = swap_chunks([synthesis[f * pair:(f + 1) * pair] for f in range(fields)], rows)
    for i in range(lat_count):
        syn_out[i] = by_lat[i].astype(jnp.bfloat16)
    b_copies = lat_exchange(syn_out, syn, syn.at[lon, lat], b_send, b_recv)
    for copy in b_copies:
        copy.start()
    syn[lon, lat] = syn_out[lat]
    for copy in b_copies:
        copy.wait_recv()
    c_copies = lon_gather(syn, c_send, c_recv)
    for copy in c_copies:
        copy.start()

    def back(j):
        stacked = syn[j].reshape(block, fields * rows)
        contract = (((0,), (0,)), ((), ()))
        return lax.dot_general(
            stacked, inverse_table[0, j], contract, preferred_element_type=jnp.float32
        ) + lax.dot_general(stacked, inverse_table[1, j], contract, preferred_element_type=jnp.float32)

    load = back(lon)
    for d in range(1, lon_count):
        c_copies[d - 1].wait_recv()
        load = load + back(source(d))
    wet_own = wet_in[...].astype(jnp.float32)
    for f in range(fields):
        part = load[f * rows:(f + 1) * rows]
        total[f] = stepped[0, f] + wet_own * part[:, :cols]
        loading[f] = part[:, cols:]

    def h_copies(up):
        here = pl.ds(0, EDGE) if up else pl.ds(rows - EDGE, EDGE)
        there = pl.ds(0, EDGE) if up else pl.ds(EDGE, EDGE)
        k = 0 if up else 1
        at = lat - 1 if up else lat + 1
        return [remote(total.at[:, here], rh3.at[:, there], h_send.at[k], h_recv.at[k], at, lon)]

    on_sides(h_copies, start, start)
    for copy in p_copies:
        copy.wait_recv()
    wait_recv_sides(w_copies)
    wait_recv_sides(h_copies)
    rlon2[:, rows:, :] = jnp.zeros((2, 2 * EDGE, cols), jnp.float32)

    @pl.loop(0, fields)
    def _(f):
        keep, half, depth, wet = coef[0], coef[1], coef[2], coef[3]
        height = assemble(total[f], rh3[f], rlon2[0], rlon2[1], f)
        none = jnp.zeros((2 * EDGE, cols), jnp.float32)
        beyond = jnp.concatenate([loading[f], none], axis=0)
        beyond = jnp.concatenate([jnp.zeros((ext_rows, cols), jnp.float32), beyond], axis=1)
        height = height + wet * beyond
        east = assemble(stepped[1, f], none, rlon2[0], rlon2[1], f + fields)
        north = assemble(stepped[2, f], rw2[f], jnp.zeros((ext_rows, cols), jnp.float32), jnp.zeros((ext_rows, cols), jnp.float32), 0)
        height, east, north = step_on_tile(height, east, north, keep, half, depth)
        out_h[f] = height[:rows, :cols]
        out_u[f] = east[:rows, :cols]
        out_w[f] = north[:rows, :cols]

    on_sides(lat_copies, wait_send, wait_send)
    on_sides(w_copies, wait_send, wait_send)
    on_sides(h_copies, wait_send, wait_send)
    for copy in lon_copies + g_copies + p_copies + a_copies + b_copies + c_copies:
        copy.wait_send()


def fused(misfit, flow_east, flow_north, ocean_depth, drag_rate, wet_mask, legendre, love_factor, assignment):
    fields, rows, cols = misfit.shape
    lat_count = lax.axis_size("lat")
    lon_count = lax.axis_size("lon")
    slots, lats, degrees = legendre.shape
    orders = lon_count * cols // 2
    used = min(degrees, orders)
    pair = 2 * slots
    block = lat_count * pair
    f32, b16 = jnp.float32, jnp.bfloat16
    ext_rows = rows + 2 * EDGE
    tile = jax.ShapeDtypeStruct((fields, rows, cols), f32)
    vmem = pl.BlockSpec(memory_space=pltpu.VMEM)
    dma = pltpu.SemaphoreType.DMA
    return pl.pallas_call(
        lambda *refs: fused_kernel(lat_count, lon_count, *refs),
        out_shape=(tile, tile, tile),
        in_specs=[vmem] * 6 + [pl.BlockSpec(memory_space=pl.ANY)] + [vmem] * 2,
        out_specs=(vmem, vmem, vmem),
        scratch_shapes=[
            pltpu.VMEM((slots, lats, used), b16),
            pltpu.VMEM((2, 2, rows, cols), f32),
            pltpu.VMEM((2, 2, ext_rows, cols), f32),
            pltpu.VMEM((3, fields, 2 * EDGE, cols), f32),
            pltpu.VMEM((2 * EDGE, cols), f32),
            pltpu.VMEM((2 * EDGE, cols), f32),
            pltpu.VMEM((2 * EDGE, cols), jnp.int32),
            pltpu.VMEM((4, ext_rows, 2 * cols), f32),
            pltpu.VMEM((3, fields, rows, cols), f32),
            pltpu.VMEM((lon_count, fields * rows, cols), b16),
            pltpu.VMEM((lon_count, 2 * block, cols), b16),
            pltpu.VMEM((2, lon_count, block, 2 * cols), b16),
            pltpu.VMEM((2 * orders, 1), jnp.int32),
            pltpu.VMEM((slots, used), f32),
            pltpu.VMEM((lat_count, pair, fields * rows), b16),
            pltpu.VMEM((lat_count, pair, fields * rows), b16),
            pltpu.VMEM((lat_count, pair, fields * rows), b16),
            pltpu.VMEM((lon_count, lat_count, pair, fields * rows), b16),
            pltpu.VMEM((2, 1, rows, cols), f32),
            pltpu.VMEM((2, ext_rows, cols), f32),
            pltpu.VMEM((fields, 2 * EDGE, cols), f32),
            pltpu.VMEM((fields, rows, cols), f32),
            pltpu.VMEM((fields, 2 * EDGE, cols), f32),
            pltpu.VMEM((fields, rows, cols), f32),
            dma,
            dma((2, 6)), dma((2, 6)), dma((2,)), dma((2,)), dma((4,)), dma((4,)),
            dma((lon_count - 1,)), dma((lon_count - 1,)),
            dma((lat_count - 1,)), dma((lat_count - 1,)), dma((lat_count - 1,)), dma((lat_count - 1,)),
            dma((lon_count - 1,)), dma((lon_count - 1,)),
            dma((2,)), dma((2,)), dma((2,)), dma((2,)), dma((2,)), dma((2,)),
        ],
        compiler_params=pltpu.CompilerParams(
            collective_id=0, has_side_effects=True, vmem_limit_bytes=40 * 1024 * 1024
        ),
    )(
        misfit, flow_east, flow_north, ocean_depth, drag_rate, wet_mask, legendre,
        love_factor.reshape(1, -1), assignment.reshape(1, -1),
    )


def whole(*arrays):
    misfit, legendre = arrays[0], arrays[6]
    fields, rows, cols = misfit.shape
    lat_count = lax.axis_size("lat")
    lon_count = lax.axis_size("lon")
    fits = (
        fields == lat_count
        and legendre.shape[0] % 8 == 0
        and cols == 16 * EDGE
        and fields * EDGE * 2 <= cols
        and rows % 32 == 0
        and lon_count > 2
        and (cols * lon_count) & (cols * lon_count - 1) == 0
    )
    return fused(*arrays) if fits else local(*arrays)


def solution(mesh):
    placed = (
        P(None, "lat", "lon"),
        P(None, "lat", "lon"),
        P(None, "lat", "lon"),
        P("lat", "lon"),
        P("lat", "lon"),
        P("lat", "lon"),
        P(("lon", "lat"), None, None),
        P(),
        P(),
    )
    return jax.shard_map(
        whole,
        mesh=mesh,
        in_specs=placed,
        out_specs=(P(None, "lat", "lon"), P(None, "lat", "lon"), P(None, "lat", "lon")),
        check_vma=False,
    )
```

```python
import math

import jax
import jax.numpy as jnp
from jax import lax
from jax.experimental import pallas as pl
from jax.experimental.pallas import tpu as pltpu
from jax.sharding import PartitionSpec as P

TIME_STEPS = 4


TWO_PI = 2.0 * math.pi
exact_mode = lax.Precision.HIGHEST


def with_halo(cells, sides, width):
    for axis, dim in sides:
        count = lax.axis_size(axis)
        head = lax.slice_in_dim(cells, 0, width, axis=dim)
        tail = lax.slice_in_dim(cells, cells.shape[dim] - width, cells.shape[dim], axis=dim)
        cells = jnp.concatenate(
            [
                lax.ppermute(tail, axis, [(i, (i + 1) % count) for i in range(count)]),
                cells,
                lax.ppermute(head, axis, [((i + 1) % count, i) for i in range(count)]),
            ],
            axis=dim,
        )
    return cells


def extend(stacked):
    return with_halo(stacked, (("lat", 2), ("lon", 3)), 1)


def differences(extended):
    east_diff = extended[:, :, 1:-1, 2:] - extended[:, :, 1:-1, :-2]
    north_diff = extended[:, :, 2:, 1:-1] - extended[:, :, :-2, 1:-1]
    return (east_diff, north_diff)


def adjoint_step(height, east_flow, north_flow, wetness, ocean_depth, drag_rate):
    east_diff, north_diff = differences(extend(height[None]))
    retained = 1.0 - drag_rate
    east_flow = wetness * (retained * east_flow - 0.5 * east_diff[0])
    north_flow = wetness * (retained * north_flow - 0.5 * north_diff[0])
    flow_east_diff, flow_north_diff = differences(extend(jnp.stack([east_flow, north_flow])))
    height = wetness * (height - 0.5 * ocean_depth * (flow_east_diff[0] + flow_north_diff[1]))
    return (height, east_flow, north_flow)


def phases(orders, positions, period):
    products = orders[:, None] * positions[None, :] % period
    radians = products.astype(jnp.float32) * (TWO_PI / period)
    return (jnp.cos(radians), jnp.sin(radians))


def spherical(spectra, legendre, weights, lat_count, row_count):
    slot_count = legendre.shape[0]
    degree_count = legendre.shape[2]
    legendre_blocks = legendre.reshape(slot_count, lat_count, row_count, degree_count)
    spectra_blocks = spectra.reshape(slot_count, lat_count, -1, row_count)
    coefficients = jnp.einsum(
        "kicr,kirn->kcn", spectra_blocks, legendre_blocks, preferred_element_type=jnp.float32
    )
    coefficients = (coefficients * weights[:, None, :]).astype(jnp.bfloat16)
    synthesis = jnp.einsum(
        "kcn,kirn->kicr", coefficients, legendre_blocks, preferred_element_type=jnp.float32
    )
    return synthesis.astype(jnp.bfloat16)


def local(
    misfit,
    flow_east,
    flow_north,
    ocean_depth,
    drag_rate,
    wet_mask,
    legendre,
    love_factor,
    assignment,
):
    field_count, row_count, col_count = misfit.shape
    lat_count = lax.axis_size("lat")
    lon_count = lax.axis_size("lon")
    period = col_count * lon_count
    order_count = period // 2
    slot_count = legendre.shape[0]
    degree_count = legendre.shape[2]
    row_pair = row_count // lon_count
    lat_index = lax.axis_index("lat")
    lon_index = lax.axis_index("lon")
    wetness = wet_mask.astype(jnp.float32)
    height = wetness * misfit
    east_flow = wetness * flow_east
    north_flow = wetness * flow_north

    def advance(height, east_flow, north_flow):
        return adjoint_step(height, east_flow, north_flow, wetness, ocean_depth, drag_rate)

    for _ in range(TIME_STEPS):
        height, east_flow, north_flow = advance(height, east_flow, north_flow)
    base = (lon_index * lat_count + lat_index) * slot_count
    my_orders = lax.dynamic_slice_in_dim(assignment, base, slot_count)
    love_pad = jnp.concatenate([love_factor, jnp.zeros((degree_count,), jnp.float32)])
    weights = jax.vmap(
        lambda first_order: lax.dynamic_slice_in_dim(love_pad, first_order, degree_count)
    )(my_orders)
    all_cells = jnp.arange(period, dtype=jnp.int32)
    cos_full, sin_full = phases(assignment, all_cells, period)
    row_block = lax.all_to_all(height, "lon", split_axis=1, concat_axis=2, tiled=True)
    real_part = jnp.einsum("nrx,mx->nrm", row_block, cos_full, precision=exact_mode)
    imag_part = -jnp.einsum("nrx,mx->nrm", row_block, sin_full, precision=exact_mode)
    rowwise = jnp.stack([real_part, imag_part], 2).astype(jnp.bfloat16)
    gathered = rowwise.transpose(3, 2, 0, 1).reshape(lon_count, lat_count, -1)
    received = lax.all_to_all(
        lax.all_to_all(gathered, "lat", split_axis=1, concat_axis=1, tiled=True),
        "lon",
        split_axis=0,
        concat_axis=0,
        tiled=True,
    )
    received = received.reshape(lon_count, lat_count, slot_count, 2, field_count, row_pair)
    spectra = received.transpose(2, 1, 3, 4, 0, 5).reshape(
        slot_count, lat_count, 2 * field_count * row_count
    )
    synthesis = spherical(spectra, legendre, weights, lat_count, row_count)
    arranged = synthesis.reshape(slot_count, lat_count, 2, field_count, lon_count, row_pair)
    arranged = arranged.transpose(4, 1, 0, 2, 3, 5).reshape(lon_count, lat_count, -1)
    returned = lax.all_to_all(
        lax.all_to_all(arranged, "lat", split_axis=1, concat_axis=1, tiled=True),
        "lon",
        split_axis=0,
        concat_axis=0,
        tiled=True,
    )
    returned = returned.reshape(order_count, 2, field_count, row_pair).astype(jnp.float32)
    doubling = jnp.where(assignment == 0, 1.0, 2.0).astype(jnp.float32)
    grid_rows = jnp.einsum(
        "mx,mfr->frx", cos_full * doubling[:, None], returned[:, 0], precision=exact_mode
    ) - jnp.einsum(
        "mx,mfr->frx", sin_full * doubling[:, None], returned[:, 1], precision=exact_mode
    )
    loading = lax.all_to_all(grid_rows, "lon", split_axis=2, concat_axis=1, tiled=True)
    height = height + wetness * loading
    return advance(height, east_flow, north_flow)


EDGE = 8
MESH = pl.DeviceIdType.MESH


def turn(value, shift, axis):
    size = value.shape[axis]
    return pltpu.roll(value, shift % size, axis)


def step_on_tile(height, east, north, keep, half, depth):
    east_diff = turn(height, -1, 1) - turn(height, 1, 1)
    north_diff = turn(height, -1, 0) - turn(height, 1, 0)
    east = keep * east - half * east_diff
    north = keep * north - half * north_diff
    spread = (turn(east, -1, 1) - turn(east, 1, 1)) + (turn(north, -1, 0) - turn(north, 1, 0))
    return height - depth * spread, east, north


def unit_cosine(counts, period):
    part = (counts & (period - 1)).astype(jnp.float32) * (1.0 / period)
    angle = (jnp.abs(part - 0.5) - 0.25) * TWO_PI
    square = angle * angle
    series = -1.0 / 39916800.0
    for denominator in (362880.0, -5040.0, 120.0, -6.0, 1.0):
        series = series * square + 1.0 / denominator
    return series * angle


def split_pair(value):
    high = value.astype(jnp.bfloat16)
    return high, (value - high.astype(jnp.float32)).astype(jnp.bfloat16)


def swap_chunks(parts, width):
    count = len(parts)
    lane = lax.broadcasted_iota(jnp.int32, parts[0].shape, 1) // width
    parts = list(parts)
    distance = 1
    while distance < count:
        upper = (lane // distance) % 2 == 1
        for low in range(count):
            if (low // distance) % 2 == 0:
                first, second = parts[low], parts[low + distance]
                parts[low] = jnp.where(upper, turn(second, width * distance, 1), first)
                parts[low + distance] = jnp.where(upper, second, turn(first, -width * distance, 1))
        distance *= 2
    return parts


def fused_kernel(
    lat_count, lon_count, misfit_far, east_far, north_far, depth_far, drag_far, wet_far, table_in, love_far,
    order_far, out_h, out_u, out_w, table, pack, rlon, rlat, rdepth, rdrag, rwet, coef, stepped, gath,
    forward_table, inverse_table, order_col, weights, spec_out, spec_in, syn_out, syn, pack2, rlon2,
    rw2, total, rh3, loading, own, depth_in, drag_in, wet_in, love_in, order_in, own_sem, table_sem, lat_send, lat_recv, lon_send, lon_recv, diag_send, diag_recv,
    g_send, g_recv, a_send, a_recv, b_send, b_recv, c_send, c_recv, w_send, w_recv, p_send, p_recv,
    h_send, h_recv,
):
    misfit, flow_east, flow_north = own.at[0], own.at[1], own.at[2]
    fields, rows, cols = misfit_far.shape
    slots = table.shape[0]
    used = table.shape[2]
    period = cols * lon_count
    ext_rows, ext_cols = rows + 2 * EDGE, 2 * cols
    pair = 2 * slots
    lat, lon = lax.axis_index("lat"), lax.axis_index("lon")
    last = lat_count - 1
    has_up, has_down = lat > 0, lat < last
    left, right = lax.rem(lon + lon_count - 1, lon_count), lax.rem(lon + 1, lon_count)
    own_copies = [
        pltpu.make_async_copy(far, near, own_sem.at[n])
        for n, (far, near) in enumerate(
            [
                (misfit_far, misfit), (east_far, flow_east), (north_far, flow_north), (depth_far, depth_in),
                (drag_far, drag_in), (wet_far, wet_in), (love_far, love_in), (order_far, order_in),
            ]
        )
    ]
    for copy in own_copies:
        copy.start()
    table_copy = pltpu.make_async_copy(table_in.at[:, :, pl.ds(0, used)], table, table_sem)
    barrier = pltpu.get_barrier_semaphore()

    def hello(at_lat, at_lon):
        pl.semaphore_signal(barrier, inc=1, device_id={"lat": at_lat, "lon": at_lon}, device_id_type=MESH)

    @pl.when(lat == 0)
    def _():
        rlat[:, :, EDGE:, :] = jnp.zeros((3, fields, EDGE, cols), jnp.float32)
        rdepth[EDGE:, :] = jnp.zeros((EDGE, cols), jnp.float32)
        rdrag[EDGE:, :] = jnp.zeros((EDGE, cols), jnp.float32)
        rwet[EDGE:, :] = jnp.zeros((EDGE, cols), jnp.int32)
        rlon[:, :, rows + EDGE:, :] = jnp.zeros((2, 2, EDGE, cols), jnp.float32)
        rw2[:, EDGE:, :] = jnp.zeros((fields, EDGE, cols), jnp.float32)
        rh3[:, EDGE:, :] = jnp.zeros((fields, EDGE, cols), jnp.float32)

    @pl.when(lat == last)
    def _():
        rlat[:, :, :EDGE, :] = jnp.zeros((3, fields, EDGE, cols), jnp.float32)
        rdepth[:EDGE, :] = jnp.zeros((EDGE, cols), jnp.float32)
        rdrag[:EDGE, :] = jnp.zeros((EDGE, cols), jnp.float32)
        rwet[:EDGE, :] = jnp.zeros((EDGE, cols), jnp.int32)
        rlon[:, :, rows:rows + EDGE, :] = jnp.zeros((2, 2, EDGE, cols), jnp.float32)
        rw2[:, :EDGE, :] = jnp.zeros((fields, EDGE, cols), jnp.float32)
        rh3[:, :EDGE, :] = jnp.zeros((fields, EDGE, cols), jnp.float32)

    for d in range(1, lat_count):
        hello(lax.rem(lat + d, lat_count), lon)
    for d in range(1, lon_count):
        hello(lat, lax.rem(lon + d, lon_count))

    @pl.when(has_up)
    def _():
        hello(lat - 1, left)
        hello(lat - 1, right)

    @pl.when(has_down)
    def _():
        hello(lat + 1, left)
        hello(lat + 1, right)

    lane_own = lax.broadcasted_iota(jnp.int32, (rows, cols), 1)

    def pack_edges(groups, target):
        for t, group in enumerate(groups):
            heads = jnp.zeros((rows, cols), jnp.float32)
            tails = jnp.zeros((rows, cols), jnp.float32)
            for s, value in enumerate(group):
                here = lane_own // EDGE == s
                heads = jnp.where(here, turn(value, EDGE * s, 1), heads)
                tails = jnp.where(here, turn(value, EDGE * s + EDGE, 1), tails)
            target[0, t] = heads
            target[1, t] = tails

    for copy in own_copies:
        copy.wait()
    table_copy.start()
    pack_edges(
        (
            [misfit[f] for f in range(fields)] + [flow_east[f] for f in range(fields)],
            [flow_north[f] for f in range(fields)]
            + [depth_in[...], drag_in[...], wet_in[...].astype(jnp.float32)],
        ),
        pack,
    )
    sides = has_up.astype(jnp.int32) + has_down.astype(jnp.int32)
    pl.semaphore_wait(barrier, lat_count + lon_count - 2 + 2 * sides)

    def remote(source, target, send, recv, at_lat, at_lon):
        return pltpu.make_async_remote_copy(
            src_ref=source, dst_ref=target, send_sem=send, recv_sem=recv,
            device_id={"lat": at_lat, "lon": at_lon}, device_id_type=MESH,
        )

    def lat_copies(up):
        here = pl.ds(0, EDGE) if up else pl.ds(rows - EDGE, EDGE)
        there = pl.ds(0, EDGE) if up else pl.ds(EDGE, EDGE)
        at = lat - 1 if up else lat + 1
        k = 0 if up else 1
        pairs = [
            (misfit_far.at[:, here], rlat.at[0, :, there]),
            (east_far.at[:, here], rlat.at[1, :, there]),
            (north_far.at[:, here], rlat.at[2, :, there]),
            (depth_far.at[here], rdepth.at[there]),
            (drag_far.at[here], rdrag.at[there]),
            (wet_far.at[here], rwet.at[there]),
        ]
        copies = [
            remote(s, t, lat_send.at[k, n], lat_recv.at[k, n], at, lon) for n, (s, t) in enumerate(pairs)
        ]
        corner = pl.ds(rows, EDGE) if up else pl.ds(rows + EDGE, EDGE)
        for side, at_lon in ((0, left), (1, right)):
            n = 2 * k + side
            copies.append(
                remote(
                    pack.at[side, :, here], rlon.at[side, :, corner], diag_send.at[n], diag_recv.at[n], at, at_lon
                )
            )
        return copies

    lon_copies = [
        remote(pack.at[s], rlon.at[s, :, pl.ds(0, rows)], lon_send.at[s], lon_recv.at[s], lat, at)
        for s, at in ((0, left), (1, right))
    ]

    def on_sides(make, act_up, act_down):
        @pl.when(has_up)
        def _():
            for copy in make(True):
                act_up(copy)

        @pl.when(has_down)
        def _():
            for copy in make(False):
                act_down(copy)

    def start(copy):
        copy.start()

    def wait_send(copy):
        copy.wait_send()

    def wait_recv_sides(make):
        @pl.when(has_down)
        def _():
            for copy in make(True):
                copy.wait_recv()

        @pl.when(has_up)
        def _():
            for copy in make(False):
                copy.wait_recv()

    on_sides(lat_copies, start, start)
    for copy in lon_copies:
        copy.start()

    orders = period // 2
    span = 2 * orders
    row_id = lax.broadcasted_iota(jnp.int32, (span, orders), 0) // 2
    position_id = lax.broadcasted_iota(jnp.int32, (span, orders), 1)
    chosen = jnp.where(row_id == position_id, order_in[...].astype(jnp.float32), 0.0)
    order_col[...] = jnp.sum(chosen, axis=1, keepdims=True).astype(jnp.int32)

    block = lat_count * pair
    parity = (lax.broadcasted_iota(jnp.int32, (block, ext_cols), 0) % 2) * (period // 4)
    lane_ext = lax.broadcasted_iota(jnp.int32, (block, ext_cols), 1)
    shifted = jnp.where(lane_ext < cols + cols // 2, lane_ext, lane_ext - ext_cols) + lon * cols
    for j in range(lon_count):
        order_here = order_col[pl.ds(j * block, block), :]
        value = unit_cosine(order_here * shifted + parity, period)
        value = value * jnp.where(order_here == 0, 1.0, 2.0)
        inverse_table[0, j], inverse_table[1, j] = split_pair(value)
    mine = order_col[pl.ds(pl.multiple_of(lon * block, block), block), :]
    lane_full = lax.broadcasted_iota(jnp.int32, (block, cols), 1)
    for j in range(lon_count):
        value = unit_cosine(mine * (lane_full + j * cols) + parity[:, :cols], period)
        forward_table[j, 0:block], forward_table[j, block:] = split_pair(value)

    degree_row = lax.broadcasted_iota(jnp.int32, (orders, used), 0)
    degree_lane = lax.broadcasted_iota(jnp.int32, (orders, used), 1)
    diagonal = lax.broadcasted_iota(jnp.int32, (orders, orders), 0) == lax.broadcasted_iota(
        jnp.int32, (orders, orders), 1
    )
    love_col = jnp.sum(jnp.where(diagonal, love_in[...], 0.0), axis=1, keepdims=True)
    offset = degree_row - degree_lane
    first = (lon * lat_count + lat) * slots
    for p in range(slots):
        order_here = order_col[pl.ds(2 * (first + p), 1), :]
        weights[p:p + 1, :] = jnp.sum(jnp.where(offset == order_here, love_col, 0.0), axis=0, keepdims=True)

    wait_recv_sides(lat_copies)
    for copy in lon_copies:
        copy.wait_recv()

    lane_tall = lax.broadcasted_iota(jnp.int32, (ext_rows, cols), 1)

    def assemble(own, beside, ahead, behind, slot):
        main = jnp.concatenate([own, beside], axis=0)
        ahead = turn_to(ahead, cols - EDGE * slot)
        behind = turn_to(behind, 2 * cols - EDGE - EDGE * slot)
        extra = jnp.where(lane_tall < EDGE, ahead, jnp.where(lane_tall >= cols - EDGE, behind, 0.0))
        return jnp.concatenate([main, extra], axis=1)

    def turn_to(value, shift):
        return pltpu.roll(value, shift % cols if isinstance(shift, int) else lax.rem(shift, cols), 1)

    depth_ext = assemble(depth_in[...], rdepth[...], rlon[0, 1], rlon[1, 1], fields)
    drag_ext = assemble(drag_in[...], rdrag[...], rlon[0, 1], rlon[1, 1], fields + 1)
    wet_ext = assemble(
        wet_in[...].astype(jnp.float32), rwet[...].astype(jnp.float32), rlon[0, 1], rlon[1, 1], fields + 2
    )
    coef[0] = wet_ext * (1.0 - drag_ext)
    coef[1] = 0.5 * wet_ext
    coef[2] = 0.5 * wet_ext * depth_ext
    coef[3] = wet_ext

    @pl.loop(0, fields)
    def _(f):
        keep, half, depth, wet = coef[0], coef[1], coef[2], coef[3]
        height = wet * assemble(misfit[f], rlat[0, f], rlon[0, 0], rlon[1, 0], f)
        east = wet * assemble(flow_east[f], rlat[1, f], rlon[0, 0], rlon[1, 0], f + fields)
        north = wet * assemble(flow_north[f], rlat[2, f], rlon[0, 1], rlon[1, 1], f)
        for _ in range(TIME_STEPS):
            height, east, north = step_on_tile(height, east, north, keep, half, depth)
        height = height[:rows, :cols]
        stepped[0, f] = height
        stepped[1, f] = east[:rows, :cols]
        stepped[2, f] = north[:rows, :cols]
        gath[lon, pl.ds(pl.multiple_of(f * rows, rows), rows), :] = height.astype(jnp.bfloat16)

    def lon_gather(ref, send, recv):
        return [
            remote(ref.at[lon], ref.at[lon], send.at[d - 1], recv.at[d - 1], lat, lax.rem(lon + d, lon_count))
            for d in range(1, lon_count)
        ]

    def source(d):
        return lax.rem(lon + lon_count - d, lon_count)

    g_copies = lon_gather(gath, g_send, g_recv)
    for copy in g_copies:
        copy.start()

    pack_edges(([stepped[k, f] for k in range(2) for f in range(fields)],), pack2)

    def w_copies(up):
        here = pl.ds(0, EDGE) if up else pl.ds(rows - EDGE, EDGE)
        there = pl.ds(0, EDGE) if up else pl.ds(EDGE, EDGE)
        k = 0 if up else 1
        at = lat - 1 if up else lat + 1
        return [remote(stepped.at[2, :, here], rw2.at[:, there], w_send.at[k], w_recv.at[k], at, lon)]

    p_copies = [
        remote(pack2.at[s, 0], rlon2.at[s, pl.ds(0, rows)], p_send.at[s], p_recv.at[s], lat, at)
        for s, at in ((0, left), (1, right))
    ]

    def transform(j):
        return lax.dot_general(
            forward_table[j], gath[j], (((1,), (1,)), ((), ())), preferred_element_type=jnp.float32
        )

    both = transform(lon)
    for d in range(1, lon_count):
        g_copies[d - 1].wait_recv()
        both = both + transform(source(d))
    spectra = (both[:block] + both[block:]).astype(jnp.bfloat16)
    for i in range(lat_count):
        spec_out[i] = spectra[i * pair:(i + 1) * pair]

    def lat_exchange(ref, target, slot, send, recv):
        copies = []
        for d in range(1, lat_count):
            peer = lax.rem(lat + d, lat_count)
            copies.append(remote(ref.at[peer], slot, send.at[d - 1], recv.at[d - 1], peer, lon))
        return copies

    a_copies = lat_exchange(spec_out, spec_in, spec_in.at[lat], a_send, a_recv)
    for copy in a_copies:
        copy.start()
    on_sides(w_copies, start, start)
    for copy in p_copies:
        copy.start()
    spec_in[lat] = spec_out[lat]
    table_copy.wait()
    for copy in a_copies:
        copy.wait_recv()
    by_field = swap_chunks([spec_in[i].astype(jnp.float32) for i in range(lat_count)], rows)
    arranged = jnp.concatenate(by_field, axis=0).astype(jnp.bfloat16)
    slot_of_row = (lax.broadcasted_iota(jnp.int32, (fields * pair, used), 0) // 2) % slots
    coefficients = jnp.zeros((fields * pair, used), jnp.float32)
    for p in range(slots):
        product = jnp.dot(arranged, table[p], preferred_element_type=jnp.float32)
        coefficients = jnp.where(slot_of_row == p, product * weights[p:p + 1, :], coefficients)
    synthesis = jnp.zeros((fields * pair, table.shape[1]), jnp.float32)
    for p in range(slots):
        synthesis = synthesis + lax.dot_general(
            jnp.where(slot_of_row == p, coefficients, 0.0).astype(jnp.bfloat16),
            table[p],
            (((1,), (1,)), ((), ())),
            preferred_element_type=jnp.float32,
        )
    by_lat = swap_chunks([synthesis[f * pair:(f + 1) * pair] for f in range(fields)], rows)
    for i in range(lat_count):
        syn_out[i] = by_lat[i].astype(jnp.bfloat16)
    b_copies = lat_exchange(syn_out, syn, syn.at[lon, lat], b_send, b_recv)
    for copy in b_copies:
        copy.start()
    syn[lon, lat] = syn_out[lat]
    c_copies = []
    for e in range(lat_count):
        from_lat = lax.rem(lat + lat_count - e, lat_count)
        if e:
            b_copies[e - 1].wait_recv()
        for d in range(1, lon_count):
            copy = remote(
                syn.at[lon, from_lat], syn.at[lon, from_lat], c_send.at[d - 1, e], c_recv.at[d - 1, e],
                lat, lax.rem(lon + d, lon_count),
            )
            copy.start()
            c_copies.append(copy)

    def back(j):
        stacked = syn[j].reshape(block, fields * rows)
        contract = (((0,), (0,)), ((), ()))
        return lax.dot_general(
            stacked, inverse_table[0, j], contract, preferred_element_type=jnp.float32
        ) + lax.dot_general(stacked, inverse_table[1, j], contract, preferred_element_type=jnp.float32)

    load = back(lon)
    for d in range(1, lon_count):
        for e in range(lat_count):
            c_copies[e * (lon_count - 1) + d - 1].wait_recv()
        load = load + back(source(d))
    wet_own = wet_in[...].astype(jnp.float32)
    for f in range(fields):
        part = load[f * rows:(f + 1) * rows]
        total[f] = stepped[0, f] + wet_own * part[:, :cols]
        loading[f] = part[:, cols:]

    def h_copies(up):
        here = pl.ds(0, EDGE) if up else pl.ds(rows - EDGE, EDGE)
        there = pl.ds(0, EDGE) if up else pl.ds(EDGE, EDGE)
        k = 0 if up else 1
        at = lat - 1 if up else lat + 1
        return [remote(total.at[:, here], rh3.at[:, there], h_send.at[k], h_recv.at[k], at, lon)]

    on_sides(h_copies, start, start)
    for copy in p_copies:
        copy.wait_recv()
    wait_recv_sides(w_copies)
    wait_recv_sides(h_copies)
    rlon2[:, rows:, :] = jnp.zeros((2, 2 * EDGE, cols), jnp.float32)

    @pl.loop(0, fields)
    def _(f):
        keep, half, depth, wet = coef[0], coef[1], coef[2], coef[3]
        height = assemble(total[f], rh3[f], rlon2[0], rlon2[1], f)
        none = jnp.zeros((2 * EDGE, cols), jnp.float32)
        beyond = jnp.concatenate([loading[f], none], axis=0)
        beyond = jnp.concatenate([jnp.zeros((ext_rows, cols), jnp.float32), beyond], axis=1)
        height = height + wet * beyond
        east = assemble(stepped[1, f], none, rlon2[0], rlon2[1], f + fields)
        north = assemble(stepped[2, f], rw2[f], jnp.zeros((ext_rows, cols), jnp.float32), jnp.zeros((ext_rows, cols), jnp.float32), 0)
        height, east, north = step_on_tile(height, east, north, keep, half, depth)
        out_h[f] = height[:rows, :cols]
        out_u[f] = east[:rows, :cols]
        out_w[f] = north[:rows, :cols]

    on_sides(lat_copies, wait_send, wait_send)
    on_sides(w_copies, wait_send, wait_send)
    on_sides(h_copies, wait_send, wait_send)
    for copy in lon_copies + g_copies + p_copies + a_copies + b_copies + c_copies:
        copy.wait_send()


def fused(misfit, flow_east, flow_north, ocean_depth, drag_rate, wet_mask, legendre, love_factor, assignment):
    fields, rows, cols = misfit.shape
    lat_count = lax.axis_size("lat")
    lon_count = lax.axis_size("lon")
    slots, lats, degrees = legendre.shape
    orders = lon_count * cols // 2
    used = min(degrees, orders)
    pair = 2 * slots
    block = lat_count * pair
    f32, b16 = jnp.float32, jnp.bfloat16
    ext_rows = rows + 2 * EDGE
    tile = jax.ShapeDtypeStruct((fields, rows, cols), f32)
    vmem = pl.BlockSpec(memory_space=pltpu.VMEM)
    dma = pltpu.SemaphoreType.DMA
    return pl.pallas_call(
        lambda *refs: fused_kernel(lat_count, lon_count, *refs),
        out_shape=(tile, tile, tile),
        in_specs=[pl.BlockSpec(memory_space=pltpu.HBM)] * 9,
        out_specs=(vmem, vmem, vmem),
        scratch_shapes=[
            pltpu.VMEM((slots, lats, used), b16),
            pltpu.VMEM((2, 2, rows, cols), f32),
            pltpu.VMEM((2, 2, ext_rows, cols), f32),
            pltpu.VMEM((3, fields, 2 * EDGE, cols), f32),
            pltpu.VMEM((2 * EDGE, cols), f32),
            pltpu.VMEM((2 * EDGE, cols), f32),
            pltpu.VMEM((2 * EDGE, cols), jnp.int32),
            pltpu.VMEM((4, ext_rows, 2 * cols), f32),
            pltpu.VMEM((3, fields, rows, cols), f32),
            pltpu.VMEM((lon_count, fields * rows, cols), b16),
            pltpu.VMEM((lon_count, 2 * block, cols), b16),
            pltpu.VMEM((2, lon_count, block, 2 * cols), b16),
            pltpu.VMEM((2 * orders, 1), jnp.int32),
            pltpu.VMEM((slots, used), f32),
            pltpu.VMEM((lat_count, pair, fields * rows), b16),
            pltpu.VMEM((lat_count, pair, fields * rows), b16),
            pltpu.VMEM((lat_count, pair, fields * rows), b16),
            pltpu.VMEM((lon_count, lat_count, pair, fields * rows), b16),
            pltpu.VMEM((2, 1, rows, cols), f32),
            pltpu.VMEM((2, ext_rows, cols), f32),
            pltpu.VMEM((fields, 2 * EDGE, cols), f32),
            pltpu.VMEM((fields, rows, cols), f32),
            pltpu.VMEM((fields, 2 * EDGE, cols), f32),
            pltpu.VMEM((fields, rows, cols), f32),
            pltpu.VMEM((3, fields, rows, cols), f32),
            pltpu.VMEM((rows, cols), f32),
            pltpu.VMEM((rows, cols), f32),
            pltpu.VMEM((rows, cols), jnp.int32),
            pltpu.VMEM((1, orders), f32),
            pltpu.VMEM((1, orders), jnp.int32),
            dma((8,)),
            dma,
            dma((2, 6)), dma((2, 6)), dma((2,)), dma((2,)), dma((4,)), dma((4,)),
            dma((lon_count - 1,)), dma((lon_count - 1,)),
            dma((lat_count - 1,)), dma((lat_count - 1,)), dma((lat_count - 1,)), dma((lat_count - 1,)),
            dma((lon_count - 1, lat_count)), dma((lon_count - 1, lat_count)),
            dma((2,)), dma((2,)), dma((2,)), dma((2,)), dma((2,)), dma((2,)),
        ],
        compiler_params=pltpu.CompilerParams(
            collective_id=0, has_side_effects=True, vmem_limit_bytes=67043328
        ),
    )(
        misfit, flow_east, flow_north, ocean_depth, drag_rate, wet_mask, legendre,
        love_factor.reshape(1, -1), assignment.reshape(1, -1),
    )


def whole(*arrays):
    misfit, legendre = arrays[0], arrays[6]
    fields, rows, cols = misfit.shape
    lat_count = lax.axis_size("lat")
    lon_count = lax.axis_size("lon")
    fits = (
        fields == lat_count
        and legendre.shape[0] % 8 == 0
        and cols == 16 * EDGE
        and fields * EDGE * 2 <= cols
        and rows % 32 == 0
        and lon_count > 2
        and (cols * lon_count) & (cols * lon_count - 1) == 0
    )
    return fused(*arrays) if fits else local(*arrays)


def solution(mesh):
    placed = (
        P(None, "lat", "lon"),
        P(None, "lat", "lon"),
        P(None, "lat", "lon"),
        P("lat", "lon"),
        P("lat", "lon"),
        P("lat", "lon"),
        P(("lon", "lat"), None, None),
        P(),
        P(),
    )
    return jax.shard_map(
        whole,
        mesh=mesh,
        in_specs=placed,
        out_specs=(P(None, "lat", "lon"), P(None, "lat", "lon"), P(None, "lat", "lon")),
        check_vma=False,
    )
```

```python
import math

import jax
import jax.numpy as jnp
from jax import lax
from jax.experimental import pallas as pl
from jax.experimental.pallas import tpu as pltpu
from jax.sharding import PartitionSpec as P

TIME_STEPS = 4


TWO_PI = 2.0 * math.pi
exact_mode = lax.Precision.HIGHEST


def with_halo(cells, sides, width):
    for axis, dim in sides:
        count = lax.axis_size(axis)
        head = lax.slice_in_dim(cells, 0, width, axis=dim)
        tail = lax.slice_in_dim(cells, cells.shape[dim] - width, cells.shape[dim], axis=dim)
        cells = jnp.concatenate(
            [
                lax.ppermute(tail, axis, [(i, (i + 1) % count) for i in range(count)]),
                cells,
                lax.ppermute(head, axis, [((i + 1) % count, i) for i in range(count)]),
            ],
            axis=dim,
        )
    return cells


def extend(stacked):
    return with_halo(stacked, (("lat", 2), ("lon", 3)), 1)


def differences(extended):
    east_diff = extended[:, :, 1:-1, 2:] - extended[:, :, 1:-1, :-2]
    north_diff = extended[:, :, 2:, 1:-1] - extended[:, :, :-2, 1:-1]
    return (east_diff, north_diff)


def adjoint_step(height, east_flow, north_flow, wetness, ocean_depth, drag_rate):
    east_diff, north_diff = differences(extend(height[None]))
    retained = 1.0 - drag_rate
    east_flow = wetness * (retained * east_flow - 0.5 * east_diff[0])
    north_flow = wetness * (retained * north_flow - 0.5 * north_diff[0])
    flow_east_diff, flow_north_diff = differences(extend(jnp.stack([east_flow, north_flow])))
    height = wetness * (height - 0.5 * ocean_depth * (flow_east_diff[0] + flow_north_diff[1]))
    return (height, east_flow, north_flow)


def phases(orders, positions, period):
    products = orders[:, None] * positions[None, :] % period
    radians = products.astype(jnp.float32) * (TWO_PI / period)
    return (jnp.cos(radians), jnp.sin(radians))


def spherical(spectra, legendre, weights, lat_count, row_count):
    slot_count = legendre.shape[0]
    degree_count = legendre.shape[2]
    legendre_blocks = legendre.reshape(slot_count, lat_count, row_count, degree_count)
    spectra_blocks = spectra.reshape(slot_count, lat_count, -1, row_count)
    coefficients = jnp.einsum(
        "kicr,kirn->kcn", spectra_blocks, legendre_blocks, preferred_element_type=jnp.float32
    )
    coefficients = (coefficients * weights[:, None, :]).astype(jnp.bfloat16)
    synthesis = jnp.einsum(
        "kcn,kirn->kicr", coefficients, legendre_blocks, preferred_element_type=jnp.float32
    )
    return synthesis.astype(jnp.bfloat16)


def local(
    misfit,
    flow_east,
    flow_north,
    ocean_depth,
    drag_rate,
    wet_mask,
    legendre,
    love_factor,
    assignment,
):
    field_count, row_count, col_count = misfit.shape
    lat_count = lax.axis_size("lat")
    lon_count = lax.axis_size("lon")
    period = col_count * lon_count
    order_count = period // 2
    slot_count = legendre.shape[0]
    degree_count = legendre.shape[2]
    row_pair = row_count // lon_count
    lat_index = lax.axis_index("lat")
    lon_index = lax.axis_index("lon")
    wetness = wet_mask.astype(jnp.float32)
    height = wetness * misfit
    east_flow = wetness * flow_east
    north_flow = wetness * flow_north

    def advance(height, east_flow, north_flow):
        return adjoint_step(height, east_flow, north_flow, wetness, ocean_depth, drag_rate)

    for _ in range(TIME_STEPS):
        height, east_flow, north_flow = advance(height, east_flow, north_flow)
    base = (lon_index * lat_count + lat_index) * slot_count
    my_orders = lax.dynamic_slice_in_dim(assignment, base, slot_count)
    love_pad = jnp.concatenate([love_factor, jnp.zeros((degree_count,), jnp.float32)])
    weights = jax.vmap(
        lambda first_order: lax.dynamic_slice_in_dim(love_pad, first_order, degree_count)
    )(my_orders)
    all_cells = jnp.arange(period, dtype=jnp.int32)
    cos_full, sin_full = phases(assignment, all_cells, period)
    row_block = lax.all_to_all(height, "lon", split_axis=1, concat_axis=2, tiled=True)
    real_part = jnp.einsum("nrx,mx->nrm", row_block, cos_full, precision=exact_mode)
    imag_part = -jnp.einsum("nrx,mx->nrm", row_block, sin_full, precision=exact_mode)
    rowwise = jnp.stack([real_part, imag_part], 2).astype(jnp.bfloat16)
    gathered = rowwise.transpose(3, 2, 0, 1).reshape(lon_count, lat_count, -1)
    received = lax.all_to_all(
        lax.all_to_all(gathered, "lat", split_axis=1, concat_axis=1, tiled=True),
        "lon",
        split_axis=0,
        concat_axis=0,
        tiled=True,
    )
    received = received.reshape(lon_count, lat_count, slot_count, 2, field_count, row_pair)
    spectra = received.transpose(2, 1, 3, 4, 0, 5).reshape(
        slot_count, lat_count, 2 * field_count * row_count
    )
    synthesis = spherical(spectra, legendre, weights, lat_count, row_count)
    arranged = synthesis.reshape(slot_count, lat_count, 2, field_count, lon_count, row_pair)
    arranged = arranged.transpose(4, 1, 0, 2, 3, 5).reshape(lon_count, lat_count, -1)
    returned = lax.all_to_all(
        lax.all_to_all(arranged, "lat", split_axis=1, concat_axis=1, tiled=True),
        "lon",
        split_axis=0,
        concat_axis=0,
        tiled=True,
    )
    returned = returned.reshape(order_count, 2, field_count, row_pair).astype(jnp.float32)
    doubling = jnp.where(assignment == 0, 1.0, 2.0).astype(jnp.float32)
    grid_rows = jnp.einsum(
        "mx,mfr->frx", cos_full * doubling[:, None], returned[:, 0], precision=exact_mode
    ) - jnp.einsum(
        "mx,mfr->frx", sin_full * doubling[:, None], returned[:, 1], precision=exact_mode
    )
    loading = lax.all_to_all(grid_rows, "lon", split_axis=2, concat_axis=1, tiled=True)
    height = height + wetness * loading
    return advance(height, east_flow, north_flow)


EDGE = 8
MESH = pl.DeviceIdType.MESH


def turn(value, shift, axis):
    size = value.shape[axis]
    return pltpu.roll(value, shift % size, axis)


def step_on_tile(height, east, north, keep, half, depth):
    east_diff = turn(height, -1, 1) - turn(height, 1, 1)
    north_diff = turn(height, -1, 0) - turn(height, 1, 0)
    east = keep * east - half * east_diff
    north = keep * north - half * north_diff
    spread = (turn(east, -1, 1) - turn(east, 1, 1)) + (turn(north, -1, 0) - turn(north, 1, 0))
    return height - depth * spread, east, north


def unit_cosine(counts, period):
    part = (counts & (period - 1)).astype(jnp.float32) * (1.0 / period)
    angle = (jnp.abs(part - 0.5) - 0.25) * TWO_PI
    square = angle * angle
    series = -1.0 / 39916800.0
    for denominator in (362880.0, -5040.0, 120.0, -6.0, 1.0):
        series = series * square + 1.0 / denominator
    return series * angle


def split_pair(value):
    high = value.astype(jnp.bfloat16)
    return high, (value - high.astype(jnp.float32)).astype(jnp.bfloat16)


def swap_chunks(parts, width):
    count = len(parts)
    lane = lax.broadcasted_iota(jnp.int32, parts[0].shape, 1) // width
    parts = list(parts)
    distance = 1
    while distance < count:
        upper = (lane // distance) % 2 == 1
        for low in range(count):
            if (low // distance) % 2 == 0:
                first, second = parts[low], parts[low + distance]
                parts[low] = jnp.where(upper, turn(second, width * distance, 1), first)
                parts[low + distance] = jnp.where(upper, second, turn(first, -width * distance, 1))
        distance *= 2
    return parts


def fused_kernel(
    lat_count, lon_count, misfit_far, east_far, north_far, depth_far, drag_far, wet_far, table_in, love_far,
    order_far, out, table, pack, rlon, rlat, rdepth, rdrag, rwet, coef, stepped, gath,
    forward_table, inverse_table, order_col, weights, spec_out, spec_in, syn_out, syn, pack2, rlon2,
    rw2, total, rh3, loading, own, depth_in, drag_in, wet_in, love_in, order_in, own_sem, table_sem, lat_send, lat_recv, lon_send, lon_recv, diag_send, diag_recv,
    g_send, g_recv, a_send, a_recv, b_send, b_recv, c_send, c_recv, w_send, w_recv, p_send, p_recv,
    h_send, h_recv,
):
    misfit, flow_east, flow_north = own.at[0], own.at[1], own.at[2]
    fields, rows, cols = misfit_far.shape
    slots = table.shape[0]
    used = table.shape[2]
    period = cols * lon_count
    ext_rows, ext_cols = rows + 2 * EDGE, 2 * cols
    pair = 2 * slots
    lat, lon = lax.axis_index("lat"), lax.axis_index("lon")
    last = lat_count - 1
    has_up, has_down = lat > 0, lat < last
    left, right = lax.rem(lon + lon_count - 1, lon_count), lax.rem(lon + 1, lon_count)
    own_copies = [
        pltpu.make_async_copy(far, near, own_sem.at[n])
        for n, (far, near) in enumerate(
            [
                (misfit_far, misfit), (east_far, flow_east), (north_far, flow_north), (depth_far, depth_in),
                (drag_far, drag_in), (wet_far, wet_in), (love_far, love_in), (order_far, order_in),
            ]
        )
    ]
    for copy in own_copies:
        copy.start()
    table_copy = pltpu.make_async_copy(table_in.at[:, :, pl.ds(0, used)], table, table_sem)
    barrier = pltpu.get_barrier_semaphore()

    def hello(at_lat, at_lon):
        pl.semaphore_signal(barrier, inc=1, device_id={"lat": at_lat, "lon": at_lon}, device_id_type=MESH)

    @pl.when(lat == 0)
    def _():
        rlat[:, :, EDGE:, :] = jnp.zeros((3, fields, EDGE, cols), jnp.float32)
        rdepth[EDGE:, :] = jnp.zeros((EDGE, cols), jnp.float32)
        rdrag[EDGE:, :] = jnp.zeros((EDGE, cols), jnp.float32)
        rwet[EDGE:, :] = jnp.zeros((EDGE, cols), jnp.int32)
        rlon[:, :, rows + EDGE:, :] = jnp.zeros((2, 2, EDGE, cols), jnp.float32)
        rw2[:, EDGE:, :] = jnp.zeros((fields, EDGE, cols), jnp.float32)
        rh3[:, EDGE:, :] = jnp.zeros((fields, EDGE, cols), jnp.float32)

    @pl.when(lat == last)
    def _():
        rlat[:, :, :EDGE, :] = jnp.zeros((3, fields, EDGE, cols), jnp.float32)
        rdepth[:EDGE, :] = jnp.zeros((EDGE, cols), jnp.float32)
        rdrag[:EDGE, :] = jnp.zeros((EDGE, cols), jnp.float32)
        rwet[:EDGE, :] = jnp.zeros((EDGE, cols), jnp.int32)
        rlon[:, :, rows:rows + EDGE, :] = jnp.zeros((2, 2, EDGE, cols), jnp.float32)
        rw2[:, :EDGE, :] = jnp.zeros((fields, EDGE, cols), jnp.float32)
        rh3[:, :EDGE, :] = jnp.zeros((fields, EDGE, cols), jnp.float32)

    for d in range(1, lat_count):
        hello(lax.rem(lat + d, lat_count), lon)
    for d in range(1, lon_count):
        hello(lat, lax.rem(lon + d, lon_count))

    @pl.when(has_up)
    def _():
        hello(lat - 1, left)
        hello(lat - 1, right)

    @pl.when(has_down)
    def _():
        hello(lat + 1, left)
        hello(lat + 1, right)

    lane_own = lax.broadcasted_iota(jnp.int32, (rows, cols), 1)

    def pack_edges(groups, target):
        for t, group in enumerate(groups):
            heads = jnp.zeros((rows, cols), jnp.float32)
            tails = jnp.zeros((rows, cols), jnp.float32)
            for s, value in enumerate(group):
                here = lane_own // EDGE == s
                heads = jnp.where(here, turn(value, EDGE * s, 1), heads)
                tails = jnp.where(here, turn(value, EDGE * s + EDGE, 1), tails)
            target[0, t] = heads
            target[1, t] = tails

    for copy in own_copies:
        copy.wait()
    table_copy.start()
    pack_edges(
        (
            [misfit[f] for f in range(fields)] + [flow_east[f] for f in range(fields)],
            [flow_north[f] for f in range(fields)]
            + [depth_in[...], drag_in[...], wet_in[...].astype(jnp.float32)],
        ),
        pack,
    )
    sides = has_up.astype(jnp.int32) + has_down.astype(jnp.int32)
    pl.semaphore_wait(barrier, lat_count + lon_count - 2 + 2 * sides)

    def remote(source, target, send, recv, at_lat, at_lon):
        return pltpu.make_async_remote_copy(
            src_ref=source, dst_ref=target, send_sem=send, recv_sem=recv,
            device_id={"lat": at_lat, "lon": at_lon}, device_id_type=MESH,
        )

    def lat_copies(up):
        here = pl.ds(0, EDGE) if up else pl.ds(rows - EDGE, EDGE)
        there = pl.ds(0, EDGE) if up else pl.ds(EDGE, EDGE)
        at = lat - 1 if up else lat + 1
        k = 0 if up else 1
        pairs = [
            (misfit_far.at[:, here], rlat.at[0, :, there]),
            (east_far.at[:, here], rlat.at[1, :, there]),
            (north_far.at[:, here], rlat.at[2, :, there]),
            (depth_far.at[here], rdepth.at[there]),
            (drag_far.at[here], rdrag.at[there]),
            (wet_far.at[here], rwet.at[there]),
        ]
        copies = [
            remote(s, t, lat_send.at[k, n], lat_recv.at[k, n], at, lon) for n, (s, t) in enumerate(pairs)
        ]
        corner = pl.ds(rows, EDGE) if up else pl.ds(rows + EDGE, EDGE)
        for side, at_lon in ((0, left), (1, right)):
            n = 2 * k + side
            copies.append(
                remote(
                    pack.at[side, :, here], rlon.at[side, :, corner], diag_send.at[n], diag_recv.at[n], at, at_lon
                )
            )
        return copies

    lon_copies = [
        remote(pack.at[s], rlon.at[s, :, pl.ds(0, rows)], lon_send.at[s], lon_recv.at[s], lat, at)
        for s, at in ((0, left), (1, right))
    ]

    def on_sides(make, act_up, act_down):
        @pl.when(has_up)
        def _():
            for copy in make(True):
                act_up(copy)

        @pl.when(has_down)
        def _():
            for copy in make(False):
                act_down(copy)

    def start(copy):
        copy.start()

    def wait_send(copy):
        copy.wait_send()

    def wait_recv_sides(make):
        @pl.when(has_down)
        def _():
            for copy in make(True):
                copy.wait_recv()

        @pl.when(has_up)
        def _():
            for copy in make(False):
                copy.wait_recv()

    on_sides(lat_copies, start, start)
    for copy in lon_copies:
        copy.start()

    orders = period // 2
    span = 2 * orders
    row_id = lax.broadcasted_iota(jnp.int32, (span, orders), 0) // 2
    position_id = lax.broadcasted_iota(jnp.int32, (span, orders), 1)
    chosen = jnp.where(row_id == position_id, order_in[...].astype(jnp.float32), 0.0)
    order_col[...] = jnp.sum(chosen, axis=1, keepdims=True).astype(jnp.int32)

    block = lat_count * pair
    parity = (lax.broadcasted_iota(jnp.int32, (block, ext_cols), 0) % 2) * (period // 4)
    lane_ext = lax.broadcasted_iota(jnp.int32, (block, ext_cols), 1)
    shifted = jnp.where(lane_ext < cols + cols // 2, lane_ext, lane_ext - ext_cols) + lon * cols
    for j in range(lon_count):
        order_here = order_col[pl.ds(j * block, block), :]
        value = unit_cosine(order_here * shifted + parity, period)
        value = value * jnp.where(order_here == 0, 1.0, 2.0)
        inverse_table[0, j], inverse_table[1, j] = split_pair(value)
    mine = order_col[pl.ds(pl.multiple_of(lon * block, block), block), :]
    lane_full = lax.broadcasted_iota(jnp.int32, (block, cols), 1)
    for j in range(lon_count):
        value = unit_cosine(mine * (lane_full + j * cols) + parity[:, :cols], period)
        forward_table[j, 0:block], forward_table[j, block:] = split_pair(value)

    degree_row = lax.broadcasted_iota(jnp.int32, (orders, used), 0)
    degree_lane = lax.broadcasted_iota(jnp.int32, (orders, used), 1)
    diagonal = lax.broadcasted_iota(jnp.int32, (orders, orders), 0) == lax.broadcasted_iota(
        jnp.int32, (orders, orders), 1
    )
    love_col = jnp.sum(jnp.where(diagonal, love_in[...], 0.0), axis=1, keepdims=True)
    offset = degree_row - degree_lane
    first = (lon * lat_count + lat) * slots
    for p in range(slots):
        order_here = order_col[pl.ds(2 * (first + p), 1), :]
        weights[p:p + 1, :] = jnp.sum(jnp.where(offset == order_here, love_col, 0.0), axis=0, keepdims=True)

    wait_recv_sides(lat_copies)
    for copy in lon_copies:
        copy.wait_recv()

    lane_tall = lax.broadcasted_iota(jnp.int32, (ext_rows, cols), 1)

    def assemble(own, beside, ahead, behind, slot):
        main = jnp.concatenate([own, beside], axis=0)
        ahead = turn_to(ahead, cols - EDGE * slot)
        behind = turn_to(behind, 2 * cols - EDGE - EDGE * slot)
        extra = jnp.where(lane_tall < EDGE, ahead, jnp.where(lane_tall >= cols - EDGE, behind, 0.0))
        return jnp.concatenate([main, extra], axis=1)

    def turn_to(value, shift):
        return pltpu.roll(value, shift % cols if isinstance(shift, int) else lax.rem(shift, cols), 1)

    depth_ext = assemble(depth_in[...], rdepth[...], rlon[0, 1], rlon[1, 1], fields)
    drag_ext = assemble(drag_in[...], rdrag[...], rlon[0, 1], rlon[1, 1], fields + 1)
    wet_ext = assemble(
        wet_in[...].astype(jnp.float32), rwet[...].astype(jnp.float32), rlon[0, 1], rlon[1, 1], fields + 2
    )
    coef[0] = wet_ext * (1.0 - drag_ext)
    coef[1] = 0.5 * wet_ext
    coef[2] = 0.5 * wet_ext * depth_ext
    coef[3] = wet_ext

    def advance_field(f):
        keep, half, depth, wet = coef[0], coef[1], coef[2], coef[3]
        height = wet * assemble(misfit[f], rlat[0, f], rlon[0, 0], rlon[1, 0], f)
        east = wet * assemble(flow_east[f], rlat[1, f], rlon[0, 0], rlon[1, 0], f + fields)
        north = wet * assemble(flow_north[f], rlat[2, f], rlon[0, 1], rlon[1, 1], f)
        for _ in range(TIME_STEPS):
            height, east, north = step_on_tile(height, east, north, keep, half, depth)
        height = height[:rows, :cols]
        stepped[0, f] = height
        stepped[1, f] = east[:rows, :cols]
        stepped[2, f] = north[:rows, :cols]
        gath[lon, pl.ds(pl.multiple_of(f * rows, rows), rows), :] = height.astype(jnp.bfloat16)

    halves = fields // 2
    g_copies = []
    for part in range(2):
        pl.loop(part * halves, (part + 1) * halves)(advance_field)
        span_rows = pl.ds(part * halves * rows, halves * rows)
        for d in range(1, lon_count):
            copy = remote(
                gath.at[lon, span_rows], gath.at[lon, span_rows], g_send.at[part, d - 1],
                g_recv.at[part, d - 1], lat, lax.rem(lon + d, lon_count),
            )
            copy.start()
            g_copies.append(copy)

    def source(d):
        return lax.rem(lon + lon_count - d, lon_count)

    pack_edges(([stepped[k, f] for k in range(2) for f in range(fields)],), pack2)

    def w_copies(up):
        here = pl.ds(0, EDGE) if up else pl.ds(rows - EDGE, EDGE)
        there = pl.ds(0, EDGE) if up else pl.ds(EDGE, EDGE)
        k = 0 if up else 1
        at = lat - 1 if up else lat + 1
        return [remote(stepped.at[2, :, here], rw2.at[:, there], w_send.at[k], w_recv.at[k], at, lon)]

    p_copies = [
        remote(pack2.at[s, 0], rlon2.at[s, pl.ds(0, rows)], p_send.at[s], p_recv.at[s], lat, at)
        for s, at in ((0, left), (1, right))
    ]

    def transform(j):
        return lax.dot_general(
            forward_table[j], gath[j], (((1,), (1,)), ((), ())), preferred_element_type=jnp.float32
        )

    both = transform(lon)
    for d in range(1, lon_count):
        g_copies[d - 1].wait_recv()
        g_copies[lon_count - 1 + d - 1].wait_recv()
        both = both + transform(source(d))
    spectra = (both[:block] + both[block:]).astype(jnp.bfloat16)
    for i in range(lat_count):
        spec_out[i] = spectra[i * pair:(i + 1) * pair]

    def lat_exchange(ref, target, slot, send, recv):
        copies = []
        for d in range(1, lat_count):
            peer = lax.rem(lat + d, lat_count)
            copies.append(remote(ref.at[peer], slot, send.at[d - 1], recv.at[d - 1], peer, lon))
        return copies

    a_copies = lat_exchange(spec_out, spec_in, spec_in.at[lat], a_send, a_recv)
    for copy in a_copies:
        copy.start()
    on_sides(w_copies, start, start)
    for copy in p_copies:
        copy.start()
    spec_in[lat] = spec_out[lat]
    table_copy.wait()
    for copy in a_copies:
        copy.wait_recv()
    by_field = swap_chunks([spec_in[i].astype(jnp.float32) for i in range(lat_count)], rows)
    arranged = jnp.concatenate(by_field, axis=0).astype(jnp.bfloat16)
    slot_of_row = (lax.broadcasted_iota(jnp.int32, (fields * pair, used), 0) // 2) % slots
    coefficients = jnp.zeros((fields * pair, used), jnp.float32)
    for p in range(slots):
        product = jnp.dot(arranged, table[p], preferred_element_type=jnp.float32)
        coefficients = jnp.where(slot_of_row == p, product * weights[p:p + 1, :], coefficients)
    synthesis = jnp.zeros((fields * pair, table.shape[1]), jnp.float32)
    for p in range(slots):
        synthesis = synthesis + lax.dot_general(
            jnp.where(slot_of_row == p, coefficients, 0.0).astype(jnp.bfloat16),
            table[p],
            (((1,), (1,)), ((), ())),
            preferred_element_type=jnp.float32,
        )
    by_lat = swap_chunks([synthesis[f * pair:(f + 1) * pair] for f in range(fields)], rows)
    for i in range(lat_count):
        syn_out[i] = by_lat[i].astype(jnp.bfloat16)
    b_copies = lat_exchange(syn_out, syn, syn.at[lon, lat], b_send, b_recv)
    for copy in b_copies:
        copy.start()
    syn[lon, lat] = syn_out[lat]
    c_copies = []
    for e in range(lat_count):
        from_lat = lax.rem(lat + lat_count - e, lat_count)
        if e:
            b_copies[e - 1].wait_recv()
        for d in range(1, lon_count):
            copy = remote(
                syn.at[lon, from_lat], syn.at[lon, from_lat], c_send.at[d - 1, e], c_recv.at[d - 1, e],
                lat, lax.rem(lon + d, lon_count),
            )
            copy.start()
            c_copies.append(copy)

    def back(j):
        stacked = syn[j].reshape(block, fields * rows)
        contract = (((0,), (0,)), ((), ()))
        return lax.dot_general(
            stacked, inverse_table[0, j], contract, preferred_element_type=jnp.float32
        ) + lax.dot_general(stacked, inverse_table[1, j], contract, preferred_element_type=jnp.float32)

    load = back(lon)
    for d in range(1, lon_count):
        for e in range(lat_count):
            c_copies[e * (lon_count - 1) + d - 1].wait_recv()
        load = load + back(source(d))
    wet_own = wet_in[...].astype(jnp.float32)
    for f in range(fields):
        part = load[f * rows:(f + 1) * rows]
        total[f] = stepped[0, f] + wet_own * part[:, :cols]
        loading[f] = part[:, cols:]

    def h_copies(up):
        here = pl.ds(0, EDGE) if up else pl.ds(rows - EDGE, EDGE)
        there = pl.ds(0, EDGE) if up else pl.ds(EDGE, EDGE)
        k = 0 if up else 1
        at = lat - 1 if up else lat + 1
        return [remote(total.at[:, here], rh3.at[:, there], h_send.at[k], h_recv.at[k], at, lon)]

    on_sides(h_copies, start, start)
    for copy in p_copies:
        copy.wait_recv()
    wait_recv_sides(w_copies)
    wait_recv_sides(h_copies)
    rlon2[:, rows:, :] = jnp.zeros((2, 2 * EDGE, cols), jnp.float32)

    @pl.loop(0, fields)
    def _(f):
        keep, half, depth, wet = coef[0], coef[1], coef[2], coef[3]
        height = assemble(total[f], rh3[f], rlon2[0], rlon2[1], f)
        none = jnp.zeros((2 * EDGE, cols), jnp.float32)
        beyond = jnp.concatenate([loading[f], none], axis=0)
        beyond = jnp.concatenate([jnp.zeros((ext_rows, cols), jnp.float32), beyond], axis=1)
        height = height + wet * beyond
        east = assemble(stepped[1, f], none, rlon2[0], rlon2[1], f + fields)
        north = assemble(stepped[2, f], rw2[f], jnp.zeros((ext_rows, cols), jnp.float32), jnp.zeros((ext_rows, cols), jnp.float32), 0)
        height, east, north = step_on_tile(height, east, north, keep, half, depth)
        out[0, f] = height[:rows, :cols]
        out[1, f] = east[:rows, :cols]
        out[2, f] = north[:rows, :cols]

    on_sides(lat_copies, wait_send, wait_send)
    on_sides(w_copies, wait_send, wait_send)
    on_sides(h_copies, wait_send, wait_send)
    for copy in lon_copies + g_copies + p_copies + a_copies + b_copies + c_copies:
        copy.wait_send()


def fused(misfit, flow_east, flow_north, ocean_depth, drag_rate, wet_mask, legendre, love_factor, assignment):
    fields, rows, cols = misfit.shape
    lat_count = lax.axis_size("lat")
    lon_count = lax.axis_size("lon")
    slots, lats, degrees = legendre.shape
    orders = lon_count * cols // 2
    used = min(degrees, orders)
    pair = 2 * slots
    block = lat_count * pair
    f32, b16 = jnp.float32, jnp.bfloat16
    ext_rows = rows + 2 * EDGE
    tiles = jax.ShapeDtypeStruct((3, fields, rows, cols), f32)
    vmem = pl.BlockSpec(memory_space=pltpu.VMEM)
    dma = pltpu.SemaphoreType.DMA
    stacked = pl.pallas_call(
        lambda *refs: fused_kernel(lat_count, lon_count, *refs),
        out_shape=tiles,
        in_specs=[pl.BlockSpec(memory_space=pltpu.HBM)] * 9,
        out_specs=vmem,
        scratch_shapes=[
            pltpu.VMEM((slots, lats, used), b16),
            pltpu.VMEM((2, 2, rows, cols), f32),
            pltpu.VMEM((2, 2, ext_rows, cols), f32),
            pltpu.VMEM((3, fields, 2 * EDGE, cols), f32),
            pltpu.VMEM((2 * EDGE, cols), f32),
            pltpu.VMEM((2 * EDGE, cols), f32),
            pltpu.VMEM((2 * EDGE, cols), jnp.int32),
            pltpu.VMEM((4, ext_rows, 2 * cols), f32),
            pltpu.VMEM((3, fields, rows, cols), f32),
            pltpu.VMEM((lon_count, fields * rows, cols), b16),
            pltpu.VMEM((lon_count, 2 * block, cols), b16),
            pltpu.VMEM((2, lon_count, block, 2 * cols), b16),
            pltpu.VMEM((2 * orders, 1), jnp.int32),
            pltpu.VMEM((slots, used), f32),
            pltpu.VMEM((lat_count, pair, fields * rows), b16),
            pltpu.VMEM((lat_count, pair, fields * rows), b16),
            pltpu.VMEM((lat_count, pair, fields * rows), b16),
            pltpu.VMEM((lon_count, lat_count, pair, fields * rows), b16),
            pltpu.VMEM((2, 1, rows, cols), f32),
            pltpu.VMEM((2, ext_rows, cols), f32),
            pltpu.VMEM((fields, 2 * EDGE, cols), f32),
            pltpu.VMEM((fields, rows, cols), f32),
            pltpu.VMEM((fields, 2 * EDGE, cols), f32),
            pltpu.VMEM((fields, rows, cols), f32),
            pltpu.VMEM((3, fields, rows, cols), f32),
            pltpu.VMEM((rows, cols), f32),
            pltpu.VMEM((rows, cols), f32),
            pltpu.VMEM((rows, cols), jnp.int32),
            pltpu.VMEM((1, orders), f32),
            pltpu.VMEM((1, orders), jnp.int32),
            dma((8,)),
            dma,
            dma((2, 6)), dma((2, 6)), dma((2,)), dma((2,)), dma((4,)), dma((4,)),
            dma((2, lon_count - 1)), dma((2, lon_count - 1)),
            dma((lat_count - 1,)), dma((lat_count - 1,)), dma((lat_count - 1,)), dma((lat_count - 1,)),
            dma((lon_count - 1, lat_count)), dma((lon_count - 1, lat_count)),
            dma((2,)), dma((2,)), dma((2,)), dma((2,)), dma((2,)), dma((2,)),
        ],
        compiler_params=pltpu.CompilerParams(
            collective_id=0, has_side_effects=True, vmem_limit_bytes=67043328
        ),
    )(
        misfit, flow_east, flow_north, ocean_depth, drag_rate, wet_mask, legendre,
        love_factor.reshape(1, -1), assignment.reshape(1, -1),
    )
    return stacked[0], stacked[1], stacked[2]


def whole(*arrays):
    misfit, legendre = arrays[0], arrays[6]
    fields, rows, cols = misfit.shape
    lat_count = lax.axis_size("lat")
    lon_count = lax.axis_size("lon")
    fits = (
        fields == lat_count
        and legendre.shape[0] % 8 == 0
        and cols == 16 * EDGE
        and fields * EDGE * 2 <= cols
        and rows % 32 == 0
        and lon_count > 2
        and (cols * lon_count) & (cols * lon_count - 1) == 0
    )
    return fused(*arrays) if fits else local(*arrays)


def solution(mesh):
    placed = (
        P(None, "lat", "lon"),
        P(None, "lat", "lon"),
        P(None, "lat", "lon"),
        P("lat", "lon"),
        P("lat", "lon"),
        P("lat", "lon"),
        P(("lon", "lat"), None, None),
        P(),
        P(),
    )
    return jax.shard_map(
        whole,
        mesh=mesh,
        in_specs=placed,
        out_specs=(P(None, "lat", "lon"), P(None, "lat", "lon"), P(None, "lat", "lon")),
        check_vma=False,
    )
```

```python
import math

import jax
import jax.numpy as jnp
from jax import lax
from jax.experimental import pallas as pl
from jax.experimental.pallas import tpu as pltpu
from jax.sharding import PartitionSpec as P

TIME_STEPS = 4


TWO_PI = 2.0 * math.pi
exact_mode = lax.Precision.HIGHEST


def with_halo(cells, sides, width):
    for axis, dim in sides:
        count = lax.axis_size(axis)
        head = lax.slice_in_dim(cells, 0, width, axis=dim)
        tail = lax.slice_in_dim(cells, cells.shape[dim] - width, cells.shape[dim], axis=dim)
        cells = jnp.concatenate(
            [
                lax.ppermute(tail, axis, [(i, (i + 1) % count) for i in range(count)]),
                cells,
                lax.ppermute(head, axis, [((i + 1) % count, i) for i in range(count)]),
            ],
            axis=dim,
        )
    return cells


def extend(stacked):
    return with_halo(stacked, (("lat", 2), ("lon", 3)), 1)


def differences(extended):
    east_diff = extended[:, :, 1:-1, 2:] - extended[:, :, 1:-1, :-2]
    north_diff = extended[:, :, 2:, 1:-1] - extended[:, :, :-2, 1:-1]
    return (east_diff, north_diff)


def adjoint_step(height, east_flow, north_flow, wetness, ocean_depth, drag_rate):
    east_diff, north_diff = differences(extend(height[None]))
    retained = 1.0 - drag_rate
    east_flow = wetness * (retained * east_flow - 0.5 * east_diff[0])
    north_flow = wetness * (retained * north_flow - 0.5 * north_diff[0])
    flow_east_diff, flow_north_diff = differences(extend(jnp.stack([east_flow, north_flow])))
    height = wetness * (height - 0.5 * ocean_depth * (flow_east_diff[0] + flow_north_diff[1]))
    return (height, east_flow, north_flow)


def phases(orders, positions, period):
    products = orders[:, None] * positions[None, :] % period
    radians = products.astype(jnp.float32) * (TWO_PI / period)
    return (jnp.cos(radians), jnp.sin(radians))


def spherical(spectra, legendre, weights, lat_count, row_count):
    slot_count = legendre.shape[0]
    degree_count = legendre.shape[2]
    legendre_blocks = legendre.reshape(slot_count, lat_count, row_count, degree_count)
    spectra_blocks = spectra.reshape(slot_count, lat_count, -1, row_count)
    coefficients = jnp.einsum(
        "kicr,kirn->kcn", spectra_blocks, legendre_blocks, preferred_element_type=jnp.float32
    )
    coefficients = (coefficients * weights[:, None, :]).astype(jnp.bfloat16)
    synthesis = jnp.einsum(
        "kcn,kirn->kicr", coefficients, legendre_blocks, preferred_element_type=jnp.float32
    )
    return synthesis.astype(jnp.bfloat16)


def local(
    misfit,
    flow_east,
    flow_north,
    ocean_depth,
    drag_rate,
    wet_mask,
    legendre,
    love_factor,
    assignment,
):
    field_count, row_count, col_count = misfit.shape
    lat_count = lax.axis_size("lat")
    lon_count = lax.axis_size("lon")
    period = col_count * lon_count
    order_count = period // 2
    slot_count = legendre.shape[0]
    degree_count = legendre.shape[2]
    row_pair = row_count // lon_count
    lat_index = lax.axis_index("lat")
    lon_index = lax.axis_index("lon")
    wetness = wet_mask.astype(jnp.float32)
    height = wetness * misfit
    east_flow = wetness * flow_east
    north_flow = wetness * flow_north

    def advance(height, east_flow, north_flow):
        return adjoint_step(height, east_flow, north_flow, wetness, ocean_depth, drag_rate)

    for _ in range(TIME_STEPS):
        height, east_flow, north_flow = advance(height, east_flow, north_flow)
    base = (lon_index * lat_count + lat_index) * slot_count
    my_orders = lax.dynamic_slice_in_dim(assignment, base, slot_count)
    love_pad = jnp.concatenate([love_factor, jnp.zeros((degree_count,), jnp.float32)])
    weights = jax.vmap(
        lambda first_order: lax.dynamic_slice_in_dim(love_pad, first_order, degree_count)
    )(my_orders)
    all_cells = jnp.arange(period, dtype=jnp.int32)
    cos_full, sin_full = phases(assignment, all_cells, period)
    row_block = lax.all_to_all(height, "lon", split_axis=1, concat_axis=2, tiled=True)
    real_part = jnp.einsum("nrx,mx->nrm", row_block, cos_full, precision=exact_mode)
    imag_part = -jnp.einsum("nrx,mx->nrm", row_block, sin_full, precision=exact_mode)
    rowwise = jnp.stack([real_part, imag_part], 2).astype(jnp.bfloat16)
    gathered = rowwise.transpose(3, 2, 0, 1).reshape(lon_count, lat_count, -1)
    received = lax.all_to_all(
        lax.all_to_all(gathered, "lat", split_axis=1, concat_axis=1, tiled=True),
        "lon",
        split_axis=0,
        concat_axis=0,
        tiled=True,
    )
    received = received.reshape(lon_count, lat_count, slot_count, 2, field_count, row_pair)
    spectra = received.transpose(2, 1, 3, 4, 0, 5).reshape(
        slot_count, lat_count, 2 * field_count * row_count
    )
    synthesis = spherical(spectra, legendre, weights, lat_count, row_count)
    arranged = synthesis.reshape(slot_count, lat_count, 2, field_count, lon_count, row_pair)
    arranged = arranged.transpose(4, 1, 0, 2, 3, 5).reshape(lon_count, lat_count, -1)
    returned = lax.all_to_all(
        lax.all_to_all(arranged, "lat", split_axis=1, concat_axis=1, tiled=True),
        "lon",
        split_axis=0,
        concat_axis=0,
        tiled=True,
    )
    returned = returned.reshape(order_count, 2, field_count, row_pair).astype(jnp.float32)
    doubling = jnp.where(assignment == 0, 1.0, 2.0).astype(jnp.float32)
    grid_rows = jnp.einsum(
        "mx,mfr->frx", cos_full * doubling[:, None], returned[:, 0], precision=exact_mode
    ) - jnp.einsum(
        "mx,mfr->frx", sin_full * doubling[:, None], returned[:, 1], precision=exact_mode
    )
    loading = lax.all_to_all(grid_rows, "lon", split_axis=2, concat_axis=1, tiled=True)
    height = height + wetness * loading
    return advance(height, east_flow, north_flow)


EDGE = 8
MESH = pl.DeviceIdType.MESH


def turn(value, shift, axis):
    size = value.shape[axis]
    return pltpu.roll(value, shift % size, axis)


def step_on_tile(height, east, north, keep, half, depth):
    east_diff = turn(height, -1, 1) - turn(height, 1, 1)
    north_diff = turn(height, -1, 0) - turn(height, 1, 0)
    east = keep * east - half * east_diff
    north = keep * north - half * north_diff
    spread = (turn(east, -1, 1) - turn(east, 1, 1)) + (turn(north, -1, 0) - turn(north, 1, 0))
    return height - depth * spread, east, north


def unit_cosine(counts, period):
    part = (counts & (period - 1)).astype(jnp.float32) * (1.0 / period)
    angle = (jnp.abs(part - 0.5) - 0.25) * TWO_PI
    square = angle * angle
    series = -1.0 / 39916800.0
    for denominator in (362880.0, -5040.0, 120.0, -6.0, 1.0):
        series = series * square + 1.0 / denominator
    return series * angle


def split_pair(value):
    high = value.astype(jnp.bfloat16)
    return high, (value - high.astype(jnp.float32)).astype(jnp.bfloat16)


def swap_chunks(parts, width):
    count = len(parts)
    lane = lax.broadcasted_iota(jnp.int32, parts[0].shape, 1) // width
    parts = list(parts)
    distance = 1
    while distance < count:
        upper = (lane // distance) % 2 == 1
        for low in range(count):
            if (low // distance) % 2 == 0:
                first, second = parts[low], parts[low + distance]
                parts[low] = jnp.where(upper, turn(second, width * distance, 1), first)
                parts[low + distance] = jnp.where(upper, second, turn(first, -width * distance, 1))
        distance *= 2
    return parts


def fused_kernel(
    lat_count, lon_count, misfit_far, east_far, north_far, depth_far, drag_far, wet_far, table_in, love_far,
    order_far, out, table, pack, rlon, rlat, rdepth, rdrag, rwet, coef, stepped, gath,
    forward_table, inverse_table, order_col, weights, spec_out, spec_in, syn_out, syn, pack2, rlon2,
    rw2, total, rh3, loading, own, depth_in, drag_in, wet_in, love_in, order_in, own_sem, table_sem, lat_send, lat_recv, lon_send, lon_recv, diag_send, diag_recv,
    g_send, g_recv, a_send, a_recv, b_send, b_recv, c_send, c_recv, w_send, w_recv, p_send, p_recv,
    h_send, h_recv,
):
    misfit, flow_east, flow_north = own.at[0], own.at[1], own.at[2]
    fields, rows, cols = misfit_far.shape
    slots = table.shape[0]
    used = table.shape[2]
    period = cols * lon_count
    ext_rows, ext_cols = rows + 2 * EDGE, 2 * cols
    pair = 2 * slots
    lat, lon = lax.axis_index("lat"), lax.axis_index("lon")
    last = lat_count - 1
    has_up, has_down = lat > 0, lat < last
    left, right = lax.rem(lon + lon_count - 1, lon_count), lax.rem(lon + 1, lon_count)
    own_copies = [
        pltpu.make_async_copy(far, near, own_sem.at[n])
        for n, (far, near) in enumerate(
            [
                (misfit_far, misfit), (east_far, flow_east), (north_far, flow_north), (depth_far, depth_in),
                (drag_far, drag_in), (wet_far, wet_in), (love_far, love_in), (order_far, order_in),
            ]
        )
    ]
    for copy in own_copies:
        copy.start()
    table_copy = pltpu.make_async_copy(table_in.at[:, :, pl.ds(0, used)], table, table_sem)
    barrier = pltpu.get_barrier_semaphore()

    def hello(at_lat, at_lon):
        pl.semaphore_signal(barrier, inc=1, device_id={"lat": at_lat, "lon": at_lon}, device_id_type=MESH)

    @pl.when(lat == 0)
    def _():
        rlat[:, :, EDGE:, :] = jnp.zeros((3, fields, EDGE, cols), jnp.float32)
        rdepth[EDGE:, :] = jnp.zeros((EDGE, cols), jnp.float32)
        rdrag[EDGE:, :] = jnp.zeros((EDGE, cols), jnp.float32)
        rwet[EDGE:, :] = jnp.zeros((EDGE, cols), jnp.int32)
        rlon[:, :, rows + EDGE:, :] = jnp.zeros((2, 2, EDGE, cols), jnp.float32)
        rw2[:, EDGE:, :] = jnp.zeros((fields, EDGE, cols), jnp.float32)
        rh3[:, EDGE:, :] = jnp.zeros((fields, EDGE, cols), jnp.float32)

    @pl.when(lat == last)
    def _():
        rlat[:, :, :EDGE, :] = jnp.zeros((3, fields, EDGE, cols), jnp.float32)
        rdepth[:EDGE, :] = jnp.zeros((EDGE, cols), jnp.float32)
        rdrag[:EDGE, :] = jnp.zeros((EDGE, cols), jnp.float32)
        rwet[:EDGE, :] = jnp.zeros((EDGE, cols), jnp.int32)
        rlon[:, :, rows:rows + EDGE, :] = jnp.zeros((2, 2, EDGE, cols), jnp.float32)
        rw2[:, :EDGE, :] = jnp.zeros((fields, EDGE, cols), jnp.float32)
        rh3[:, :EDGE, :] = jnp.zeros((fields, EDGE, cols), jnp.float32)

    for d in range(1, lat_count):
        hello(lax.rem(lat + d, lat_count), lon)
    for d in range(1, lon_count):
        hello(lat, lax.rem(lon + d, lon_count))

    @pl.when(has_up)
    def _():
        hello(lat - 1, left)
        hello(lat - 1, right)

    @pl.when(has_down)
    def _():
        hello(lat + 1, left)
        hello(lat + 1, right)

    lane_own = lax.broadcasted_iota(jnp.int32, (rows, cols), 1)

    def pack_edges(groups, target):
        for t, group in enumerate(groups):
            heads = jnp.zeros((rows, cols), jnp.float32)
            tails = jnp.zeros((rows, cols), jnp.float32)
            for s, value in enumerate(group):
                here = lane_own // EDGE == s
                heads = jnp.where(here, turn(value, EDGE * s, 1), heads)
                tails = jnp.where(here, turn(value, EDGE * s + EDGE, 1), tails)
            target[0, t] = heads
            target[1, t] = tails

    for copy in own_copies:
        copy.wait()
    table_copy.start()
    pack_edges(
        (
            [misfit[f] for f in range(fields)] + [flow_east[f] for f in range(fields)],
            [flow_north[f] for f in range(fields)]
            + [depth_in[...], drag_in[...], wet_in[...].astype(jnp.float32)],
        ),
        pack,
    )
    sides = has_up.astype(jnp.int32) + has_down.astype(jnp.int32)
    pl.semaphore_wait(barrier, lat_count + lon_count - 2 + 2 * sides)

    def remote(source, target, send, recv, at_lat, at_lon):
        return pltpu.make_async_remote_copy(
            src_ref=source, dst_ref=target, send_sem=send, recv_sem=recv,
            device_id={"lat": at_lat, "lon": at_lon}, device_id_type=MESH,
        )

    def lat_copies(up):
        here = pl.ds(0, EDGE) if up else pl.ds(rows - EDGE, EDGE)
        there = pl.ds(0, EDGE) if up else pl.ds(EDGE, EDGE)
        at = lat - 1 if up else lat + 1
        k = 0 if up else 1
        pairs = [
            (misfit_far.at[:, here], rlat.at[0, :, there]),
            (east_far.at[:, here], rlat.at[1, :, there]),
            (north_far.at[:, here], rlat.at[2, :, there]),
            (depth_far.at[here], rdepth.at[there]),
            (drag_far.at[here], rdrag.at[there]),
            (wet_far.at[here], rwet.at[there]),
        ]
        copies = [
            remote(s, t, lat_send.at[k, n], lat_recv.at[k, n], at, lon) for n, (s, t) in enumerate(pairs)
        ]
        corner = pl.ds(rows, EDGE) if up else pl.ds(rows + EDGE, EDGE)
        for side, at_lon in ((0, left), (1, right)):
            n = 2 * k + side
            copies.append(
                remote(
                    pack.at[side, :, here], rlon.at[side, :, corner], diag_send.at[n], diag_recv.at[n], at, at_lon
                )
            )
        return copies

    lon_copies = [
        remote(pack.at[s], rlon.at[s, :, pl.ds(0, rows)], lon_send.at[s], lon_recv.at[s], lat, at)
        for s, at in ((0, left), (1, right))
    ]

    def on_sides(make, act_up, act_down):
        @pl.when(has_up)
        def _():
            for copy in make(True):
                act_up(copy)

        @pl.when(has_down)
        def _():
            for copy in make(False):
                act_down(copy)

    def start(copy):
        copy.start()

    def wait_send(copy):
        copy.wait_send()

    def wait_recv_sides(make):
        @pl.when(has_down)
        def _():
            for copy in make(True):
                copy.wait_recv()

        @pl.when(has_up)
        def _():
            for copy in make(False):
                copy.wait_recv()

    on_sides(lat_copies, start, start)
    for copy in lon_copies:
        copy.start()

    orders = period // 2
    span = 2 * orders
    row_id = lax.broadcasted_iota(jnp.int32, (span, orders), 0) // 2
    position_id = lax.broadcasted_iota(jnp.int32, (span, orders), 1)
    chosen = jnp.where(row_id == position_id, order_in[...].astype(jnp.float32), 0.0)
    order_col[...] = jnp.sum(chosen, axis=1, keepdims=True).astype(jnp.int32)

    block = lat_count * pair
    parity = (lax.broadcasted_iota(jnp.int32, (block, ext_cols), 0) % 2) * (period // 4)
    lane_ext = lax.broadcasted_iota(jnp.int32, (block, ext_cols), 1)
    shifted = jnp.where(lane_ext < cols + cols // 2, lane_ext, lane_ext - ext_cols) + lon * cols
    for j in range(lon_count):
        order_here = order_col[pl.ds(j * block, block), :]
        value = unit_cosine(order_here * shifted + parity, period)
        value = value * jnp.where(order_here == 0, 1.0, 2.0)
        inverse_table[0, j], inverse_table[1, j] = split_pair(value)
    mine = order_col[pl.ds(pl.multiple_of(lon * block, block), block), :]
    lane_full = lax.broadcasted_iota(jnp.int32, (block, cols), 1)
    for j in range(lon_count):
        value = unit_cosine(mine * (lane_full + j * cols) + parity[:, :cols], period)
        forward_table[j, 0:block], forward_table[j, block:] = split_pair(value)

    degree_row = lax.broadcasted_iota(jnp.int32, (orders, used), 0)
    degree_lane = lax.broadcasted_iota(jnp.int32, (orders, used), 1)
    diagonal = lax.broadcasted_iota(jnp.int32, (orders, orders), 0) == lax.broadcasted_iota(
        jnp.int32, (orders, orders), 1
    )
    love_col = jnp.sum(jnp.where(diagonal, love_in[...], 0.0), axis=1, keepdims=True)
    offset = degree_row - degree_lane
    first = (lon * lat_count + lat) * slots
    for p in range(slots):
        order_here = order_col[pl.ds(2 * (first + p), 1), :]
        weights[p:p + 1, :] = jnp.sum(jnp.where(offset == order_here, love_col, 0.0), axis=0, keepdims=True)

    wait_recv_sides(lat_copies)
    for copy in lon_copies:
        copy.wait_recv()

    lane_tall = lax.broadcasted_iota(jnp.int32, (ext_rows, cols), 1)

    def assemble(own, beside, ahead, behind, slot):
        main = jnp.concatenate([own, beside], axis=0)
        ahead = turn_to(ahead, cols - EDGE * slot)
        behind = turn_to(behind, 2 * cols - EDGE - EDGE * slot)
        extra = jnp.where(lane_tall < EDGE, ahead, jnp.where(lane_tall >= cols - EDGE, behind, 0.0))
        return jnp.concatenate([main, extra], axis=1)

    def turn_to(value, shift):
        return pltpu.roll(value, shift % cols if isinstance(shift, int) else lax.rem(shift, cols), 1)

    depth_ext = assemble(depth_in[...], rdepth[...], rlon[0, 1], rlon[1, 1], fields)
    drag_ext = assemble(drag_in[...], rdrag[...], rlon[0, 1], rlon[1, 1], fields + 1)
    wet_ext = assemble(
        wet_in[...].astype(jnp.float32), rwet[...].astype(jnp.float32), rlon[0, 1], rlon[1, 1], fields + 2
    )
    coef[0] = wet_ext * (1.0 - drag_ext)
    coef[1] = 0.5 * wet_ext
    coef[2] = 0.5 * wet_ext * depth_ext
    coef[3] = wet_ext

    def advance_field(f):
        keep, half, depth, wet = coef[0], coef[1], coef[2], coef[3]
        height = wet * assemble(misfit[f], rlat[0, f], rlon[0, 0], rlon[1, 0], f)
        east = wet * assemble(flow_east[f], rlat[1, f], rlon[0, 0], rlon[1, 0], f + fields)
        north = wet * assemble(flow_north[f], rlat[2, f], rlon[0, 1], rlon[1, 1], f)
        for _ in range(TIME_STEPS):
            height, east, north = step_on_tile(height, east, north, keep, half, depth)
        height = height[:rows, :cols]
        stepped[0, f] = height
        stepped[1, f] = east[:rows, :cols]
        stepped[2, f] = north[:rows, :cols]
        gath[lon, pl.ds(pl.multiple_of(f * rows, rows), rows), :] = height.astype(jnp.bfloat16)

    parts = fields // 2
    halves = fields // parts
    g_copies = []
    for part in range(parts):
        pl.loop(part * halves, (part + 1) * halves)(advance_field)
        span_rows = pl.ds(part * halves * rows, halves * rows)
        for d in range(1, lon_count):
            copy = remote(
                gath.at[lon, span_rows], gath.at[lon, span_rows], g_send.at[part, d - 1],
                g_recv.at[part, d - 1], lat, lax.rem(lon + d, lon_count),
            )
            copy.start()
            g_copies.append(copy)

    def source(d):
        return lax.rem(lon + lon_count - d, lon_count)

    pack_edges(([stepped[k, f] for k in range(2) for f in range(fields)],), pack2)

    def w_copies(up):
        here = pl.ds(0, EDGE) if up else pl.ds(rows - EDGE, EDGE)
        there = pl.ds(0, EDGE) if up else pl.ds(EDGE, EDGE)
        k = 0 if up else 1
        at = lat - 1 if up else lat + 1
        return [remote(stepped.at[2, :, here], rw2.at[:, there], w_send.at[k], w_recv.at[k], at, lon)]

    p_copies = [
        remote(pack2.at[s, 0], rlon2.at[s, pl.ds(0, rows)], p_send.at[s], p_recv.at[s], lat, at)
        for s, at in ((0, left), (1, right))
    ]

    def transform(j):
        return lax.dot_general(
            forward_table[j], gath[j], (((1,), (1,)), ((), ())), preferred_element_type=jnp.float32
        )

    both = transform(lon)
    for d in range(1, lon_count):
        for part in range(parts):
            g_copies[part * (lon_count - 1) + d - 1].wait_recv()
        both = both + transform(source(d))
    spectra = (both[:block] + both[block:]).astype(jnp.bfloat16)
    for i in range(lat_count):
        spec_out[i] = spectra[i * pair:(i + 1) * pair]

    def lat_exchange(ref, target, slot, send, recv):
        copies = []
        for d in range(1, lat_count):
            peer = lax.rem(lat + d, lat_count)
            copies.append(remote(ref.at[peer], slot, send.at[d - 1], recv.at[d - 1], peer, lon))
        return copies

    a_copies = lat_exchange(spec_out, spec_in, spec_in.at[lat], a_send, a_recv)
    for copy in a_copies:
        copy.start()
    on_sides(w_copies, start, start)
    for copy in p_copies:
        copy.start()
    spec_in[lat] = spec_out[lat]
    table_copy.wait()
    for copy in a_copies:
        copy.wait_recv()
    by_field = swap_chunks([spec_in[i].astype(jnp.float32) for i in range(lat_count)], rows)
    arranged = jnp.concatenate(by_field, axis=0).astype(jnp.bfloat16)
    slot_of_row = (lax.broadcasted_iota(jnp.int32, (fields * pair, used), 0) // 2) % slots
    coefficients = jnp.zeros((fields * pair, used), jnp.float32)
    for p in range(slots):
        product = jnp.dot(arranged, table[p], preferred_element_type=jnp.float32)
        coefficients = jnp.where(slot_of_row == p, product * weights[p:p + 1, :], coefficients)
    synthesis = jnp.zeros((fields * pair, table.shape[1]), jnp.float32)
    for p in range(slots):
        synthesis = synthesis + lax.dot_general(
            jnp.where(slot_of_row == p, coefficients, 0.0).astype(jnp.bfloat16),
            table[p],
            (((1,), (1,)), ((), ())),
            preferred_element_type=jnp.float32,
        )
    by_lat = swap_chunks([synthesis[f * pair:(f + 1) * pair] for f in range(fields)], rows)
    for i in range(lat_count):
        syn_out[i] = by_lat[i].astype(jnp.bfloat16)
    b_copies = lat_exchange(syn_out, syn, syn.at[lon, lat], b_send, b_recv)
    for copy in b_copies:
        copy.start()
    syn[lon, lat] = syn_out[lat]
    c_copies = []
    for e in range(lat_count):
        from_lat = lax.rem(lat + lat_count - e, lat_count)
        if e:
            b_copies[e - 1].wait_recv()
        for d in range(1, lon_count):
            copy = remote(
                syn.at[lon, from_lat], syn.at[lon, from_lat], c_send.at[d - 1, e], c_recv.at[d - 1, e],
                lat, lax.rem(lon + d, lon_count),
            )
            copy.start()
            c_copies.append(copy)

    def back(j):
        stacked = syn[j].reshape(block, fields * rows)
        contract = (((0,), (0,)), ((), ()))
        return lax.dot_general(
            stacked, inverse_table[0, j], contract, preferred_element_type=jnp.float32
        ) + lax.dot_general(stacked, inverse_table[1, j], contract, preferred_element_type=jnp.float32)

    load = back(lon)
    for d in range(1, lon_count):
        for e in range(lat_count):
            c_copies[e * (lon_count - 1) + d - 1].wait_recv()
        load = load + back(source(d))
    wet_own = wet_in[...].astype(jnp.float32)
    for f in range(fields):
        part = load[f * rows:(f + 1) * rows]
        total[f] = stepped[0, f] + wet_own * part[:, :cols]
        loading[f] = part[:, cols:]

    def h_copies(up):
        here = pl.ds(0, EDGE) if up else pl.ds(rows - EDGE, EDGE)
        there = pl.ds(0, EDGE) if up else pl.ds(EDGE, EDGE)
        k = 0 if up else 1
        at = lat - 1 if up else lat + 1
        return [remote(total.at[:, here], rh3.at[:, there], h_send.at[k], h_recv.at[k], at, lon)]

    on_sides(h_copies, start, start)
    for copy in p_copies:
        copy.wait_recv()
    wait_recv_sides(w_copies)
    wait_recv_sides(h_copies)
    rlon2[:, rows:, :] = jnp.zeros((2, 2 * EDGE, cols), jnp.float32)

    @pl.loop(0, fields)
    def _(f):
        keep, half, depth, wet = coef[0], coef[1], coef[2], coef[3]
        height = assemble(total[f], rh3[f], rlon2[0], rlon2[1], f)
        none = jnp.zeros((2 * EDGE, cols), jnp.float32)
        beyond = jnp.concatenate([loading[f], none], axis=0)
        beyond = jnp.concatenate([jnp.zeros((ext_rows, cols), jnp.float32), beyond], axis=1)
        height = height + wet * beyond
        east = assemble(stepped[1, f], none, rlon2[0], rlon2[1], f + fields)
        north = assemble(stepped[2, f], rw2[f], jnp.zeros((ext_rows, cols), jnp.float32), jnp.zeros((ext_rows, cols), jnp.float32), 0)
        height, east, north = step_on_tile(height, east, north, keep, half, depth)
        out[0, f] = height[:rows, :cols]
        out[1, f] = east[:rows, :cols]
        out[2, f] = north[:rows, :cols]

    on_sides(lat_copies, wait_send, wait_send)
    on_sides(w_copies, wait_send, wait_send)
    on_sides(h_copies, wait_send, wait_send)
    for copy in lon_copies + g_copies + p_copies + a_copies + b_copies + c_copies:
        copy.wait_send()


def fused(misfit, flow_east, flow_north, ocean_depth, drag_rate, wet_mask, legendre, love_factor, assignment):
    fields, rows, cols = misfit.shape
    lat_count = lax.axis_size("lat")
    lon_count = lax.axis_size("lon")
    slots, lats, degrees = legendre.shape
    orders = lon_count * cols // 2
    used = min(degrees, orders)
    pair = 2 * slots
    block = lat_count * pair
    f32, b16 = jnp.float32, jnp.bfloat16
    ext_rows = rows + 2 * EDGE
    tiles = jax.ShapeDtypeStruct((3, fields, rows, cols), f32)
    vmem = pl.BlockSpec(memory_space=pltpu.VMEM)
    dma = pltpu.SemaphoreType.DMA
    stacked = pl.pallas_call(
        lambda *refs: fused_kernel(lat_count, lon_count, *refs),
        out_shape=tiles,
        in_specs=[pl.BlockSpec(memory_space=pltpu.HBM)] * 9,
        out_specs=vmem,
        scratch_shapes=[
            pltpu.VMEM((slots, lats, used), b16),
            pltpu.VMEM((2, 2, rows, cols), f32),
            pltpu.VMEM((2, 2, ext_rows, cols), f32),
            pltpu.VMEM((3, fields, 2 * EDGE, cols), f32),
            pltpu.VMEM((2 * EDGE, cols), f32),
            pltpu.VMEM((2 * EDGE, cols), f32),
            pltpu.VMEM((2 * EDGE, cols), jnp.int32),
            pltpu.VMEM((4, ext_rows, 2 * cols), f32),
            pltpu.VMEM((3, fields, rows, cols), f32),
            pltpu.VMEM((lon_count, fields * rows, cols), b16),
            pltpu.VMEM((lon_count, 2 * block, cols), b16),
            pltpu.VMEM((2, lon_count, block, 2 * cols), b16),
            pltpu.VMEM((2 * orders, 1), jnp.int32),
            pltpu.VMEM((slots, used), f32),
            pltpu.VMEM((lat_count, pair, fields * rows), b16),
            pltpu.VMEM((lat_count, pair, fields * rows), b16),
            pltpu.VMEM((lat_count, pair, fields * rows), b16),
            pltpu.VMEM((lon_count, lat_count, pair, fields * rows), b16),
            pltpu.VMEM((2, 1, rows, cols), f32),
            pltpu.VMEM((2, ext_rows, cols), f32),
            pltpu.VMEM((fields, 2 * EDGE, cols), f32),
            pltpu.VMEM((fields, rows, cols), f32),
            pltpu.VMEM((fields, 2 * EDGE, cols), f32),
            pltpu.VMEM((fields, rows, cols), f32),
            pltpu.VMEM((3, fields, rows, cols), f32),
            pltpu.VMEM((rows, cols), f32),
            pltpu.VMEM((rows, cols), f32),
            pltpu.VMEM((rows, cols), jnp.int32),
            pltpu.VMEM((1, orders), f32),
            pltpu.VMEM((1, orders), jnp.int32),
            dma((8,)),
            dma,
            dma((2, 6)), dma((2, 6)), dma((2,)), dma((2,)), dma((4,)), dma((4,)),
            dma((fields // 2, lon_count - 1)), dma((fields // 2, lon_count - 1)),
            dma((lat_count - 1,)), dma((lat_count - 1,)), dma((lat_count - 1,)), dma((lat_count - 1,)),
            dma((lon_count - 1, lat_count)), dma((lon_count - 1, lat_count)),
            dma((2,)), dma((2,)), dma((2,)), dma((2,)), dma((2,)), dma((2,)),
        ],
        compiler_params=pltpu.CompilerParams(
            collective_id=0, has_side_effects=True, vmem_limit_bytes=67043328
        ),
    )(
        misfit, flow_east, flow_north, ocean_depth, drag_rate, wet_mask, legendre,
        love_factor.reshape(1, -1), assignment.reshape(1, -1),
    )
    return stacked[0], stacked[1], stacked[2]


def whole(*arrays):
    misfit, legendre = arrays[0], arrays[6]
    fields, rows, cols = misfit.shape
    lat_count = lax.axis_size("lat")
    lon_count = lax.axis_size("lon")
    fits = (
        fields == lat_count
        and legendre.shape[0] % 8 == 0
        and cols == 16 * EDGE
        and fields * EDGE * 2 <= cols
        and rows % 32 == 0
        and lon_count > 2
        and (cols * lon_count) & (cols * lon_count - 1) == 0
    )
    return fused(*arrays) if fits else local(*arrays)


def solution(mesh):
    placed = (
        P(None, "lat", "lon"),
        P(None, "lat", "lon"),
        P(None, "lat", "lon"),
        P("lat", "lon"),
        P("lat", "lon"),
        P("lat", "lon"),
        P(("lon", "lat"), None, None),
        P(),
        P(),
    )
    return jax.shard_map(
        whole,
        mesh=mesh,
        in_specs=placed,
        out_specs=(P(None, "lat", "lon"), P(None, "lat", "lon"), P(None, "lat", "lon")),
        check_vma=False,
    )
```
